256 devices in a mesh: dcn: 2 (over core), gx: 8 (over z), gy: 16 (over x, y).
Axes of the slice: x: 4, y: 4, z: 8, core: 2. Of those that a mesh axis runs over, the one named last changes fastest.
Arguments:
- features: bfloat16 [2, 128, 256, 2, 8, 128], P('dcn', 'gx', 'gy'), may hold values from -6 to 6
- grad_out: bfloat16 [2, 128, 256, 2, 8, 128], P('dcn', 'gx', 'gy'), may hold values from -6 to 6
- occupancy: int32 [2, 128, 256, 2, 8], P('dcn', 'gx', 'gy'), may hold values from 0 to 1, as said below
- leaf_z: int32 [2, 16, 32, 2], P('dcn', 'gx', 'gy'), may hold values from -1 to 2, as said below
- neighbours: int32 [2, 16, 32, 2, 27], P('dcn', 'gx', 'gy'), may hold values from 0 to 2, as said below
- kernel: bfloat16 [27, 128, 128], replicated, may hold values from -0.15625 to 0.15625
Outputs:
- grad_features: bfloat16 [2, 128, 256, 2, 8, 128], P('dcn', 'gx', 'gy')
- kernel_grad: float32 [27, 128, 128], replicated
The draws below stay inside these ranges and needn't reach their ends.
Inputs may be any that keep to these rules, and one draw needn't show every extreme that they name: `leaf_z`: in every leaf column the active slots come first, with distinct z positions in rising order below 3; the other slots hold -1. Every scene has a leaf column with all 2 slots active. `neighbours`: for an active slot holding z position h and offset k = 9 (p + 1) + 3 (q + 1) + (r + 1), the slot of the active leaf at z position h + r in the column p, q away, or 2 if there is none; slots that are not active hold 2 at every offset. `occupancy`: zero at every voxel of a slot that is not active.
All inputs are finite; a program needn't handle non-finite values.
Results may differ from the reference program's by a relative error of at most 0.001.
Values may be sent and summed in bfloat16 or wider, within the bound.
No kernel may reach another device: no remote copies, remote signals or barrier semaphores. Data moves between devices by JAX's collectives and lax.ppermute only.
A program may use at most 64 MiB of HBM per device.

```python
import math
import jax
import jax.numpy as jnp
from jax import lax

C = 128
EDGE = 8
LEAVES = 2
DEPTH = 3
SCENES = 2
TILES_X = 16
TILES_Y = 32
NX = 128
NY = 256


def layout_tables(key):
    seeded = jax.random.fold_in(key, 4051)
    key_count, key_full, key_perm, key_mask = jax.random.split(seeded, 4)
    tile_count = SCENES * TILES_X * TILES_Y
    picked = jax.random.randint(key_count, (SCENES, TILES_X, TILES_Y), 0, LEAVES)
    filled = 1 + picked * picked // LEAVES
    full_tile = jax.random.randint(key_full, (SCENES,), 0, TILES_X * TILES_Y)
    tile_ids = jnp.arange(TILES_X * TILES_Y, dtype=jnp.int32).reshape(TILES_X, TILES_Y)
    filled = jnp.where(tile_ids[None] == full_tile[:, None, None], LEAVES, filled)
    perms = jax.vmap(lambda subkey: jax.random.permutation(subkey, DEPTH))(jax.random.split(key_perm, tile_count))
    perms = perms.reshape(SCENES, TILES_X, TILES_Y, DEPTH).astype(jnp.int32)
    slot_ids = jnp.arange(LEAVES, dtype=jnp.int32)
    filled_slot = slot_ids < filled[..., None]
    chosen = jnp.where(filled_slot, perms[..., :LEAVES], DEPTH + slot_ids)
    chosen = jnp.sort(chosen, axis=-1)
    leaf_z = jnp.where(filled_slot, chosen, -1).astype(jnp.int32)
    padded = jnp.pad(leaf_z, ((0, 0), (1, 1), (1, 1), (0, 0)), constant_values=-1)
    adjacent = []
    for step_x in (-1, 0, 1):
        for step_y in (-1, 0, 1):
            beside = padded[:, 1 + step_x:1 + step_x + TILES_X, 1 + step_y:1 + step_y + TILES_Y]
            for step_z in (-1, 0, 1):
                equals = (beside[..., None, :] == leaf_z[..., :, None] + step_z) & (beside[..., None, :] >= 0) & (leaf_z[..., :, None] >= 0)
                exists = jnp.any(equals, axis=-1)
                located = jnp.sum(jnp.where(equals, slot_ids, 0), axis=-1)
                adjacent.append(jnp.where(exists, located, LEAVES))
    neighbours = jnp.stack(adjacent, axis=-1).astype(jnp.int32)
    coin_flip = jax.random.randint(key_mask, (SCENES, NX, NY, LEAVES, EDGE), 0, 2)
    live_vox = jnp.repeat(jnp.repeat(filled_slot.astype(jnp.int32), EDGE, axis=1), EDGE, axis=2)
    occupancy = (coin_flip * live_vox[..., None]).astype(jnp.int32)
    return (leaf_z, neighbours, occupancy)


def draw_occupancy(key, part):
    return layout_tables(key)[2]


def draw_leaf_z(key, part):
    return layout_tables(key)[0]


def draw_neighbours(key, part):
    return layout_tables(key)[1]


def steps_of(key, extent, cuts, least, largest):
    level, own = 1.0, jax.random.fold_in(key, 6)
    for dim, parts in cuts:
        steps = jnp.exp(jax.random.uniform(jax.random.fold_in(own, dim), (parts,), jnp.float32, least / len(cuts), largest / len(cuts)))
        level = level * jnp.repeat(steps, extent[dim] // parts).reshape([-1 if axis == dim else 1 for axis in range(len(extent))])
    return level


def centred(stream_key, shape, deviation, limit, cuts=(), held_as=jnp.bfloat16):
    values = deviation * jax.random.normal(stream_key, shape, jnp.float32)
    if cuts:
        values = values * steps_of(stream_key, shape, cuts, -0.22, 0.18)
    return jnp.clip(values, -limit, limit).astype(held_as)


def setup_inputs(seed: int = 0) -> dict:
    streams_of = jax.random.split(jax.random.key(seed), 7)
    features = centred(streams_of[0], (SCENES, NX, NY, LEAVES, EDGE, C), 1.0, 6.0, ((0, 2), (1, 8), (2, 16)))
    grad_out = centred(streams_of[1], (SCENES, NX, NY, LEAVES, EDGE, C), 1.0, 6.0, ((0, 2), (1, 8), (2, 16)))
    occupancy = draw_occupancy(jax.random.fold_in(streams_of[6], 71), 0)
    leaf_z = draw_leaf_z(jax.random.fold_in(streams_of[6], 71), 0)
    neighbours = draw_neighbours(jax.random.fold_in(streams_of[6], 71), 0)
    kernel = centred(streams_of[5], (27, C, C), (27 * C // 2) ** -0.5, 0.15625)
    return {"features": features, "grad_out": grad_out, "occupancy": occupancy, "leaf_z": leaf_z, "neighbours": neighbours, "kernel": kernel}


def leaf_columns(padded, adjacent_row, edge):
    width = padded.shape[-1]
    spots = jnp.arange(edge + 2, dtype=jnp.int32)
    region = (spots > 0).astype(jnp.int32) + (spots > edge).astype(jnp.int32)
    base_index = region[:, None] * 9 + region[None, :] * 3
    rows_x = spots[:, None]
    rows_y = spots[None, :]
    planes = []
    for layer in range(3):
        chosen_slot = jnp.take(adjacent_row, base_index + layer)
        planes.append(padded[rows_x, rows_y, chosen_slot])
    column = jnp.concatenate([planes[0][:, :, edge - 1:], planes[1], planes[2][:, :, :1]], axis=2)
    pieces = []
    for step_x in (-1, 0, 1):
        for step_y in (-1, 0, 1):
            for step_z in (-1, 0, 1):
                pieces.append(column[1 - step_x:1 - step_x + edge, 1 - step_y:1 - step_y + edge, 1 - step_z:1 - step_z + edge])
    stacked = jnp.stack(pieces, axis=3)
    return stacked.reshape(edge * edge * edge, 27 * width)

def tile_terms(halo_zero, masked_in, keep, adjacent, active_total, wrows):
    edge = masked_in.shape[0]
    leaves = masked_in.shape[2]
    width = masked_in.shape[-1]

    def one_leaf(leaf, carry):
        grad_tile, kernel_acc = carry
        columns = leaf_columns(halo_zero, adjacent[leaf], edge)
        own = lax.dynamic_index_in_dim(masked_in, leaf, 2, keepdims=False).reshape(edge * edge * edge, width)
        leaf_keep = lax.dynamic_index_in_dim(keep, leaf, 2, keepdims=False).reshape(edge * edge * edge)
        result = jnp.dot(columns, wrows, preferred_element_type=jnp.float32) * leaf_keep[:, None].astype(jnp.float32)
        grad_tile = lax.dynamic_update_slice_in_dim(grad_tile, result.astype(jnp.bfloat16).reshape(edge, edge, 1, edge, width), leaf, 2)
        kernel_acc = kernel_acc + jnp.dot(own.T, columns, preferred_element_type=jnp.float32)
        return (grad_tile, kernel_acc)
    start = (jnp.zeros((edge, edge, leaves, edge, width), jnp.bfloat16), jnp.zeros((width, 27 * width), jnp.float32))
    return lax.fori_loop(0, active_total, one_leaf, start)

def reference(features, grad_out, occupancy, leaf_z, neighbours, kernel):
    active = (leaf_z >= 0).astype(jnp.int32)
    active_vox = jnp.repeat(jnp.repeat(active, EDGE, axis=1), EDGE, axis=2)
    keep = occupancy * active_vox[..., None]
    keep_b = keep.astype(jnp.bfloat16)[..., None]
    masked = grad_out * keep_b
    masked_in = features * keep_b
    padded = jnp.pad(masked, ((0, 0), (1, 1), (1, 1), (0, 0), (0, 0), (0, 0)))
    padded = jnp.concatenate([padded, jnp.zeros((SCENES, NX + 2, NY + 2, 1, EDGE, C), jnp.bfloat16)], axis=3)
    wrows = jnp.transpose(kernel, (0, 2, 1)).reshape(27 * C, C)
    totals = lax.optimization_barrier(jnp.sum(active, axis=-1)).astype(jnp.int32)

    def per_tile(kernel_sum, tile):
        scene = tile // (TILES_X * TILES_Y)
        tile_x = tile // TILES_Y % TILES_X
        tile_y = tile % TILES_Y
        nought = jnp.zeros((), jnp.int32)
        halo_zero = lax.dynamic_slice(padded, (scene, tile_x * EDGE, tile_y * EDGE, nought, nought, nought), (1, EDGE + 2, EDGE + 2, LEAVES + 1, EDGE, C))[0]
        own_in = lax.dynamic_slice(masked_in, (scene, tile_x * EDGE, tile_y * EDGE, nought, nought, nought), (1, EDGE, EDGE, LEAVES, EDGE, C))[0]
        own_keep = lax.dynamic_slice(keep, (scene, tile_x * EDGE, tile_y * EDGE, nought, nought), (1, EDGE, EDGE, LEAVES, EDGE))[0]
        adjacent = neighbours[scene, tile_x, tile_y]
        grad_tile, kernel_part = tile_terms(halo_zero, own_in, own_keep, adjacent, totals[scene, tile_x, tile_y], wrows)
        return (kernel_sum + kernel_part, grad_tile)
    tiles = jnp.arange(SCENES * TILES_X * TILES_Y, dtype=jnp.int32)
    kernel_sum, grads = lax.scan(per_tile, jnp.zeros((C, 27 * C), jnp.float32), tiles)
    grads = grads.reshape(SCENES, TILES_X, TILES_Y, EDGE, EDGE, LEAVES, EDGE, C)
    grads = jnp.transpose(grads, (0, 1, 3, 2, 4, 5, 6, 7)).reshape(SCENES, NX, NY, LEAVES, EDGE, C)
    scale = 1.0 / math.sqrt(SCENES * NX * NY * LEAVES * EDGE)
    kernel_grad = jnp.transpose(kernel_sum.reshape(C, 27, C), (1, 0, 2)) * scale
    return (grads, kernel_grad)
```

```python
import math

import jax
import jax.numpy as jnp
from jax import lax
from jax.experimental import pallas as pl
from jax.experimental.pallas import tpu as pltpu
from jax.sharding import PartitionSpec as P

EDGE = 8
WIDTH = 128
VIEW = EDGE + 2
ROWS = 2 * EDGE
UNIT = EDGE * EDGE * ROWS


def conv_kernel(nbr, lz, grad, feat, keep, top, bottom, left, right, wrows, out, kgrad, field, view, own, acc):
    nx, ny = grad.shape[0], grad.shape[1]
    zero_y = jnp.zeros((ny + 2, EDGE, WIDTH), jnp.float32)

    def fill(x, carry):
        field[x + 1, 1 : ny + 1, 0:2] = grad[x].astype(jnp.float32) * keep[x].astype(jnp.float32)
        return carry

    lax.fori_loop(0, nx, fill, 0)
    field[0, 1 : ny + 1, 0:2] = top[0].astype(jnp.float32)
    field[nx + 1, 1 : ny + 1, 0:2] = bottom[0].astype(jnp.float32)

    def sides(x, carry):
        field[x, 0, 0:2] = left[x, 0].astype(jnp.float32)
        field[x, ny + 1, 0:2] = right[x, 0].astype(jnp.float32)
        field[x, :, 2] = zero_y
        return carry

    lax.fori_loop(0, nx + 2, sides, 0)
    kgrad[...] = jnp.zeros_like(kgrad)

    def view_rows(i, slot, xl, p):
        spot_x = EDGE * i + xl
        for q, (start, count) in enumerate(((0, 1), (1, EDGE), (EDGE + 1, 1))):
            parts = ([], [], [])
            row = lax.broadcasted_iota(jnp.int32, (count, EDGE, WIDTH), 1)
            for j in range(2):
                base = ((i * 2 + j) * 2 + slot) * 27 + 9 * p + 3 * q
                span = pl.ds(EDGE * j + start, count)
                below = field[spot_x, span, nbr[base]]
                here = field[spot_x, span, nbr[base + 1]]
                above = field[spot_x, span, nbr[base + 2]]
                parts[0].append(pltpu.roll(jnp.where(row == 0, above, here), EDGE - 1, 1))
                parts[1].append(here)
                parts[2].append(pltpu.roll(jnp.where(row == EDGE - 1, below, here), 1, 1))
            for c in range(3):
                view[c, xl, start : start + count] = jnp.concatenate(parts[c], axis=1).astype(jnp.bfloat16)

    def unit(step, carry):
        i = step // 2
        slot = step % 2
        live = jnp.logical_or(lz[i * 4 + slot] >= 0, lz[i * 4 + 2 + slot] >= 0)

        @pl.when(live)
        def _():
            view_rows(i, slot, 0, 0)

            def middle(xl, c2):
                view_rows(i, slot, xl, 1)
                return c2

            lax.fori_loop(1, EDGE + 1, middle, 0)
            view_rows(i, slot, EDGE + 1, 2)

            def own_rows(xl, c2):
                x = EDGE * i + xl
                pair = [
                    feat[x, EDGE * j : EDGE * j + EDGE, slot].astype(jnp.float32)
                    * keep[x, EDGE * j : EDGE * j + EDGE, slot].astype(jnp.float32)
                    for j in range(2)
                ]
                own[xl] = jnp.concatenate(pair, axis=1).astype(jnp.bfloat16).reshape(EDGE * ROWS, WIDTH)
                return c2

            lax.fori_loop(0, EDGE, own_rows, 0)
            own_t = own[...].reshape(UNIT, WIDTH).T
            acc[...] = jnp.zeros_like(acc)

            def offset(t, c2):
                a = t // 3
                b = t % 3
                pieces = [
                    view[c, pl.ds(2 - a, EDGE), pl.ds(2 - b, EDGE)].reshape(UNIT, WIDTH) for c in range(3)
                ]
                columns = jnp.concatenate(pieces, axis=1)
                weights = wrows[pl.ds(pl.multiple_of(t * 3 * WIDTH, 3 * WIDTH), 3 * WIDTH), :]
                acc[...] += jnp.dot(columns, weights, preferred_element_type=jnp.float32)
                terms = jnp.dot(own_t, columns, preferred_element_type=jnp.float32)
                for c in range(3):
                    kgrad[3 * t + c] += terms[:, c * WIDTH : (c + 1) * WIDTH]
                return c2

            lax.fori_loop(0, 9, offset, 0)

            def emit(xl, c2):
                x = EDGE * i + xl
                block = acc[pl.ds(pl.multiple_of(xl * EDGE * ROWS, EDGE * ROWS), EDGE * ROWS), :]
                block = block.reshape(EDGE, 2, EDGE, WIDTH)
                for j in range(2):
                    k = keep[x, EDGE * j : EDGE * j + EDGE, slot].astype(jnp.float32)
                    out[x, EDGE * j : EDGE * j + EDGE, slot] = (block[:, j] * k).astype(jnp.bfloat16)
                return c2

            lax.fori_loop(0, EDGE, emit, 0)

        @pl.when(jnp.logical_not(live))
        def _():
            def blank(xl, c2):
                out[EDGE * i + xl, :, slot] = jnp.zeros((ny, EDGE, WIDTH), jnp.bfloat16)
                return c2

            lax.fori_loop(0, EDGE, blank, 0)

        return carry

    lax.fori_loop(0, 4, unit, 0)


def exchange(blocks, axis):
    return lax.all_to_all(blocks, axis, 0, 0)


def spread(block, axis):
    count = lax.axis_size(axis)
    return exchange(jnp.broadcast_to(block[None], (count,) + block.shape), axis)


def reduce_terms(terms, scale):
    cores = lax.axis_size("dcn")
    wide = lax.axis_size("gy")
    rows = terms.shape[0]
    half = jnp.sum(exchange(terms.reshape(cores, rows // cores, WIDTH), "dcn"), axis=0)
    piece = jnp.sum(exchange(half.reshape(wide, rows // cores // wide, WIDTH), "gy"), axis=0)
    total = jnp.sum(spread(piece, "gx"), axis=0) * scale
    half = spread(total, "gy").reshape(rows // cores, WIDTH)
    return spread(half, "dcn").reshape(rows, WIDTH)


def local(features, grad_out, occupancy, leaf_z, neighbours, kernel):
    nx, ny = grad_out.shape[1], grad_out.shape[2]
    cols_x, cols_y = leaf_z.shape[1], leaf_z.shape[2]
    grad = grad_out[0]
    feat = features[0]
    active = (leaf_z[0] >= 0).astype(jnp.int32)
    active_vox = jnp.repeat(jnp.repeat(active, EDGE, axis=0), EDGE, axis=1)
    keep = (occupancy[0] * active_vox[..., None]).astype(jnp.bfloat16)
    keep = jnp.broadcast_to(keep[..., None], grad.shape)

    def shift(block, axis, step):
        count = lax.axis_size(axis)
        pairs = [(i, i + step) for i in range(count) if 0 <= i + step < count]
        return lax.ppermute(block, axis, pairs)

    top = shift(grad[nx - 1 :] * keep[nx - 1 :], "gx", 1)
    bottom = shift(grad[:1] * keep[:1], "gx", -1)

    def side(y):
        return jnp.concatenate(
            [top[:, y : y + 1], grad[:, y : y + 1] * keep[:, y : y + 1], bottom[:, y : y + 1]], axis=0
        )

    left = shift(side(ny - 1), "gy", 1)
    right = shift(side(0), "gy", -1)
    wrows = jnp.transpose(kernel, (0, 2, 1)).reshape(27 * WIDTH, WIDTH)
    scale = 1.0 / math.sqrt(
        lax.axis_size("dcn") * lax.axis_size("gx") * lax.axis_size("gy") * nx * ny * 2 * EDGE
    )
    smem = pl.BlockSpec(memory_space=pltpu.SMEM)
    vmem = pl.BlockSpec(memory_space=pltpu.VMEM)
    out, terms = pl.pallas_call(
        conv_kernel,
        out_shape=(
            jax.ShapeDtypeStruct(grad.shape, jnp.bfloat16),
            jax.ShapeDtypeStruct((27, WIDTH, WIDTH), jnp.float32),
        ),
        in_specs=[smem, smem] + [vmem] * 8,
        out_specs=(vmem, vmem),
        scratch_shapes=[
            pltpu.VMEM((nx + 2, ny + 2, 3, EDGE, WIDTH), jnp.float32),
            pltpu.VMEM((3, VIEW, VIEW, ROWS, WIDTH), jnp.bfloat16),
            pltpu.VMEM((EDGE, EDGE * ROWS, WIDTH), jnp.bfloat16),
            pltpu.VMEM((UNIT, WIDTH), jnp.float32),
        ],
        compiler_params=pltpu.CompilerParams(vmem_limit_bytes=40 << 20),
        name="conv_backward",
    )(
        neighbours.reshape(-1),
        leaf_z.reshape(-1),
        grad,
        feat,
        keep,
        top,
        bottom,
        left,
        right,
        wrows,
    )
    kernel_grad = reduce_terms(terms.reshape(27 * WIDTH, WIDTH), scale)
    return out[None], kernel_grad.reshape(27, WIDTH, WIDTH)


def solution(mesh):
    return jax.shard_map(
        local,
        mesh=mesh,
        in_specs=(
            P("dcn", "gx", "gy", None, None, None),
            P("dcn", "gx", "gy", None, None, None),
            P("dcn", "gx", "gy", None, None),
            P("dcn", "gx", "gy", None),
            P("dcn", "gx", "gy", None, None),
            P(),
        ),
        out_specs=(P("dcn", "gx", "gy", None, None, None), P()),
        check_vma=False,
    )
```

```python
import math

import jax
import jax.numpy as jnp
from jax import lax
from jax.experimental import pallas as pl
from jax.experimental.pallas import tpu as pltpu
from jax.sharding import PartitionSpec as P

EDGE = 8
WIDTH = 128
VIEW = EDGE + 2
ROWS = 2 * EDGE
UNIT = EDGE * EDGE * ROWS
HALF = 27 * WIDTH // 2
PADDED = 1792


def fill_field(grad, keep, top, bottom, left, right, field):
    nx, ny = grad.shape[0], grad.shape[1]
    zero_y = jnp.zeros((ny + 2, EDGE, WIDTH), jnp.float32)

    def fill(x, carry):
        field[x + 1, 1 : ny + 1, 0:2] = grad[x].astype(jnp.float32) * keep[x].astype(jnp.float32)
        return carry

    lax.fori_loop(0, nx, fill, 0)
    field[0, 1 : ny + 1, 0:2] = top[0].astype(jnp.float32)
    field[nx + 1, 1 : ny + 1, 0:2] = bottom[0].astype(jnp.float32)

    def sides(x, carry):
        field[x, 0, 0:2] = left[x, 0].astype(jnp.float32)
        field[x, ny + 1, 0:2] = right[x, 0].astype(jnp.float32)
        field[x, :, 2] = zero_y
        return carry

    lax.fori_loop(0, nx + 2, sides, 0)


def fill_view(nbr, field, view, i, slot):
    def view_rows(xl, p):
        spot_x = EDGE * i + xl
        for q, (start, count) in enumerate(((0, 1), (1, EDGE), (EDGE + 1, 1))):
            parts = ([], [], [])
            row = lax.broadcasted_iota(jnp.int32, (count, EDGE, WIDTH), 1)
            for j in range(2):
                base = ((i * 2 + j) * 2 + slot) * 27 + 9 * p + 3 * q
                span = pl.ds(EDGE * j + start, count)
                below = field[spot_x, span, nbr[base]]
                here = field[spot_x, span, nbr[base + 1]]
                above = field[spot_x, span, nbr[base + 2]]
                parts[0].append(pltpu.roll(jnp.where(row == 0, above, here), EDGE - 1, 1))
                parts[1].append(here)
                parts[2].append(pltpu.roll(jnp.where(row == EDGE - 1, below, here), 1, 1))
            for c in range(3):
                view[c, xl, start : start + count] = jnp.concatenate(parts[c], axis=1).astype(jnp.bfloat16)

    view_rows(0, 0)

    def middle(xl, carry):
        view_rows(xl, 1)
        return carry

    lax.fori_loop(1, EDGE + 1, middle, 0)
    view_rows(EDGE + 1, 2)


def columns_at(view, t):
    a = t // 3
    b = t % 3
    pieces = [view[c, pl.ds(2 - a, EDGE), pl.ds(2 - b, EDGE)].reshape(UNIT, WIDTH) for c in range(3)]
    return jnp.concatenate(pieces, axis=1)


def pair_live(lz, i, slot):
    return jnp.logical_or(lz[i * 4 + slot] >= 0, lz[i * 4 + 2 + slot] >= 0)


def terms_kernel(nbr, lz, grad, feat, keep, top, bottom, left, right, terms, field, view, own):
    fill_field(grad, keep, top, bottom, left, right, field)
    terms[...] = jnp.zeros_like(terms)

    def unit(step, carry):
        i = step // 2
        slot = step % 2

        @pl.when(pair_live(lz, i, slot))
        def _():
            fill_view(nbr, field, view, i, slot)

            def own_rows(xl, c2):
                x = EDGE * i + xl
                pair = [
                    feat[x, EDGE * j : EDGE * j + EDGE, slot].astype(jnp.float32)
                    * keep[x, EDGE * j : EDGE * j + EDGE, slot].astype(jnp.float32)
                    for j in range(2)
                ]
                own[xl] = jnp.concatenate(pair, axis=1).astype(jnp.bfloat16).reshape(EDGE * ROWS, WIDTH)
                return c2

            lax.fori_loop(0, EDGE, own_rows, 0)
            own_t = own[...].reshape(UNIT, WIDTH).T

            def offset(t, c2):
                part = jnp.dot(own_t, columns_at(view, t), preferred_element_type=jnp.float32)
                for c in range(3):
                    for s in range(2):
                        half = 2 * (3 * t + c) + s
                        core = (half >= 27).astype(jnp.int32)
                        spot = pl.ds(pl.multiple_of(half * 64 - core * HALF, 64), 64)
                        terms[core, spot] += part[s * 64 : s * 64 + 64, c * WIDTH : (c + 1) * WIDTH]
                return c2

            lax.fori_loop(0, 9, offset, 0)

        return carry

    lax.fori_loop(0, 4, unit, 0)


def feature_kernel(nbr, lz, grad, keep, top, bottom, left, right, wrows, out, field, view, acc):
    ny = grad.shape[1]
    fill_field(grad, keep, top, bottom, left, right, field)

    def unit(step, carry):
        i = step // 2
        slot = step % 2
        live = pair_live(lz, i, slot)

        @pl.when(live)
        def _():
            fill_view(nbr, field, view, i, slot)
            acc[...] = jnp.zeros_like(acc)

            def offset(t, c2):
                weights = wrows[pl.ds(pl.multiple_of(t * 3 * WIDTH, 3 * WIDTH), 3 * WIDTH), :]
                acc[...] += jnp.dot(columns_at(view, t), weights, preferred_element_type=jnp.float32)
                return c2

            lax.fori_loop(0, 9, offset, 0)

            def emit(xl, c2):
                x = EDGE * i + xl
                block = acc[pl.ds(pl.multiple_of(xl * EDGE * ROWS, EDGE * ROWS), EDGE * ROWS), :]
                block = block.reshape(EDGE, 2, EDGE, WIDTH)
                for j in range(2):
                    k = keep[x, EDGE * j : EDGE * j + EDGE, slot].astype(jnp.float32)
                    out[x, EDGE * j : EDGE * j + EDGE, slot] = (block[:, j] * k).astype(jnp.bfloat16)
                return c2

            lax.fori_loop(0, EDGE, emit, 0)

        @pl.when(jnp.logical_not(live))
        def _():
            def blank(xl, c2):
                out[EDGE * i + xl, :, slot] = jnp.zeros((ny, EDGE, WIDTH), jnp.bfloat16)
                return c2

            lax.fori_loop(0, EDGE, blank, 0)

        return carry

    lax.fori_loop(0, 4, unit, 0)


def encode(value, coded, places):
    rows = value.shape[0]
    peak = jnp.max(jnp.abs(value), axis=0, keepdims=True)
    power = jnp.floor(jnp.log2(jnp.maximum(peak, 1e-30)) + 1.001)
    code = jnp.clip(jnp.round(value * jnp.exp2(15.0 - power)), -32767.0, 32767.0)
    code = code.astype(jnp.int32).astype(jnp.int16)
    power = jnp.broadcast_to(power, (EDGE, WIDTH)).astype(jnp.int32).astype(jnp.int16)
    for place in places:
        coded[place, 0:rows] = code
        coded[place, rows : rows + EDGE] = power


def decode(coded):
    rows = coded.shape[0] - EDGE
    power = coded[rows:].astype(jnp.int32).astype(jnp.float32)[0:1]
    return coded[:rows].astype(jnp.int32).astype(jnp.float32) * jnp.exp2(power - 15.0)


def encode_half_kernel(pair, coded):
    chunk = coded.shape[1] - EDGE
    for n in range(coded.shape[0]):
        spot = slice(n * chunk, n * chunk + chunk)
        encode(pair[0, spot] + pair[1, spot], coded, (n,))


def sum_kernel(scale, coded, again):
    total = decode(coded[0])
    for n in range(1, coded.shape[0]):
        total = total + decode(coded[n])
    encode(total * scale, again, range(again.shape[0]))


def decode_kernel(coded, out):
    chunk = coded.shape[2] - EDGE
    for core in range(2):
        for n in range(coded.shape[1]):
            rows = min(chunk, HALF - n * chunk)
            start = core * HALF + n * chunk
            out[start : start + rows] = decode(coded[core, n])[0:rows]


def call(kernel, name, out_shape, scratch=(), scalars=0, flops=0, nbytes=4 << 20):
    smem = pl.BlockSpec(memory_space=pltpu.SMEM)
    vmem = pl.BlockSpec(memory_space=pltpu.VMEM)

    def run(*args):
        return pl.pallas_call(
            kernel,
            out_shape=out_shape,
            in_specs=[smem] * scalars + [vmem] * (len(args) - scalars),
            out_specs=vmem,
            scratch_shapes=list(scratch),
            compiler_params=pltpu.CompilerParams(vmem_limit_bytes=40 << 20),
            cost_estimate=pl.CostEstimate(flops=flops, bytes_accessed=nbytes, transcendentals=0),
            name=name,
        )(*args)

    return run


def exchange(blocks, axis):
    return lax.all_to_all(blocks, axis, 0, 0)


def local(features, grad_out, occupancy, leaf_z, neighbours, kernel):
    nx, ny = grad_out.shape[1], grad_out.shape[2]
    grad = grad_out[0]
    feat = features[0]
    active = (leaf_z[0] >= 0).astype(jnp.int32)
    active_vox = jnp.repeat(jnp.repeat(active, EDGE, axis=0), EDGE, axis=1)
    keep = (occupancy[0] * active_vox[..., None]).astype(jnp.bfloat16)
    keep = jnp.broadcast_to(keep[..., None], grad.shape)

    def shift(block, axis, step):
        count = lax.axis_size(axis)
        pairs = [(i, i + step) for i in range(count) if 0 <= i + step < count]
        return lax.ppermute(block, axis, pairs)

    top = shift(grad[nx - 1 :] * keep[nx - 1 :], "gx", 1)
    bottom = shift(grad[:1] * keep[:1], "gx", -1)

    def side(y):
        return jnp.concatenate(
            [top[:, y : y + 1], grad[:, y : y + 1] * keep[:, y : y + 1], bottom[:, y : y + 1]], axis=0
        )

    left = shift(side(ny - 1), "gy", 1)
    right = shift(side(0), "gy", -1)
    wrows = jnp.transpose(kernel, (0, 2, 1)).reshape(27 * WIDTH, WIDTH)
    scale = 1.0 / math.sqrt(
        lax.axis_size("dcn") * lax.axis_size("gx") * lax.axis_size("gy") * nx * ny * 2 * EDGE
    )
    nbr = neighbours.reshape(-1)
    lz = leaf_z.reshape(-1)
    edges = (top, bottom, left, right)
    field = pltpu.VMEM((nx + 2, ny + 2, 3, EDGE, WIDTH), jnp.float32)
    view = pltpu.VMEM((3, VIEW, VIEW, ROWS, WIDTH), jnp.bfloat16)
    own = pltpu.VMEM((EDGE, EDGE * ROWS, WIDTH), jnp.bfloat16)
    acc = pltpu.VMEM((UNIT, WIDTH), jnp.float32)
    product = 2 * 4 * 512 * 27 * WIDTH * WIDTH

    terms = call(
        terms_kernel,
        "conv_terms",
        jax.ShapeDtypeStruct((2, PADDED, WIDTH), jnp.float32),
        (field, view, own),
        scalars=2,
        flops=product,
    )(nbr, lz, grad, feat, keep, *edges)
    pair = exchange(terms, "dcn")
    grad_late, pair = lax.optimization_barrier((grad, pair))
    out = call(
        feature_kernel,
        "conv_features",
        jax.ShapeDtypeStruct(grad.shape, jnp.bfloat16),
        (field, view, acc),
        scalars=2,
        flops=product,
    )(nbr, lz, grad_late, keep, *edges, wrows)

    gx, gy = lax.axis_size("gx"), lax.axis_size("gy")

    def coded(count):
        return jax.ShapeDtypeStruct((count, PADDED // gy + EDGE, WIDTH), jnp.int16)

    half = call(encode_half_kernel, "encode_half", coded(gy), nbytes=2 << 20)(pair)
    half = exchange(half, "gy")
    piece = call(lambda c, o: sum_kernel(1.0, c, o), "sum_piece", coded(gx), nbytes=1 << 20)(half)
    piece = exchange(piece, "gx")
    total = call(lambda c, o: sum_kernel(scale, c, o), "sum_total", coded(gy), nbytes=1 << 20)(piece)
    total = exchange(total, "gy")
    total = exchange(jnp.broadcast_to(total[None], (2,) + total.shape), "dcn")
    kernel_grad = call(
        decode_kernel, "decode_total", jax.ShapeDtypeStruct((27 * WIDTH, WIDTH), jnp.float32), nbytes=3 << 20
    )(total)
    return out[None], kernel_grad.reshape(27, WIDTH, WIDTH)


def solution(mesh):
    return jax.shard_map(
        local,
        mesh=mesh,
        in_specs=(
            P("dcn", "gx", "gy", None, None, None),
            P("dcn", "gx", "gy", None, None, None),
            P("dcn", "gx", "gy", None, None),
            P("dcn", "gx", "gy", None),
            P("dcn", "gx", "gy", None, None),
            P(),
        ),
        out_specs=(P("dcn", "gx", "gy", None, None, None), P()),
        check_vma=False,
    )
```

```python
import math

import jax
import jax.numpy as jnp
from jax import lax
from jax.experimental import pallas as pl
from jax.experimental.pallas import tpu as pltpu
from jax.sharding import PartitionSpec as P

EDGE = 8
WIDTH = 128
VIEW = EDGE + 2
ROWS = 2 * EDGE
UNIT = EDGE * EDGE * ROWS
HALF = 27 * WIDTH // 2
PADDED = 1792


def shifted(below, here, above):
    row = lax.broadcasted_iota(jnp.int32, here.shape, 1)
    return (
        pltpu.roll(jnp.where(row == 0, above, here), EDGE - 1, 1),
        here,
        pltpu.roll(jnp.where(row == EDGE - 1, below, here), 1, 1),
    )


REGIONS = ((0, 1), (1, EDGE), (EDGE + 1, 1))


def table_base(i, j, slot):
    return ((i * 2 + j) * 2 + slot) * 27


def pair_live(lz, i, slot):
    return jnp.logical_or(lz[i * 4 + slot] >= 0, lz[i * 4 + 2 + slot] >= 0)


def fill_field(i, grad, keep, edges, field):
    ny = grad.shape[1]
    low, high = (1, VIEW) if i == 0 else (0, VIEW - 1)

    def fill(r, carry):
        x = EDGE * i - 1 + r
        field[r, 1 : ny + 1, 0:2] = grad[x].astype(jnp.float32) * keep[x].astype(jnp.float32)
        return carry

    lax.fori_loop(low, high, fill, 0)
    outer = 0 if i == 0 else VIEW - 1
    field[:, :, 2] = jnp.zeros((VIEW, ny + 2, EDGE, WIDTH), jnp.float32)
    if edges is None:
        field[outer, :, 0:2] = jnp.zeros((ny + 2, 2, EDGE, WIDTH), jnp.float32)
        field[:, 0, 0:2] = jnp.zeros((VIEW, 2, EDGE, WIDTH), jnp.float32)
        field[:, ny + 1, 0:2] = jnp.zeros((VIEW, 2, EDGE, WIDTH), jnp.float32)
    else:
        top, bottom, left, right = edges
        field[outer, 1 : ny + 1, 0:2] = (top, bottom)[i][0].astype(jnp.float32)
        field[:, 0, 0:2] = left[EDGE * i : EDGE * i + VIEW, 0].astype(jnp.float32)
        field[:, ny + 1, 0:2] = right[EDGE * i : EDGE * i + VIEW, 0].astype(jnp.float32)


def fill_view(nbr, field, view, i, slot):
    def view_rows(xl, p):
        for q, (start, count) in enumerate(REGIONS):
            halves = []
            for j in range(2):
                base = table_base(i, j, slot) + 9 * p + 3 * q
                span = pl.ds(EDGE * j + start, count)
                halves.append(shifted(*(field[xl, span, nbr[base + r]] for r in range(3))))
            for c in range(3):
                both = jnp.concatenate([halves[0][c], halves[1][c]], axis=1)
                view[c, xl, start : start + count] = both.astype(jnp.bfloat16)

    view_rows(0, 0)

    def middle(xl, carry):
        view_rows(xl, 1)
        return carry

    lax.fori_loop(1, EDGE + 1, middle, 0)
    view_rows(EDGE + 1, 2)


def columns_at(view, t):
    a = t // 3
    b = t % 3
    pieces = [view[c, pl.ds(2 - a, EDGE), pl.ds(2 - b, EDGE)].reshape(UNIT, WIDTH) for c in range(3)]
    return jnp.concatenate(pieces, axis=1)


def pair_row(feat, keep, x, slot):
    pair = [
        feat[x, EDGE * j : EDGE * j + EDGE, slot].astype(jnp.float32)
        * keep[x, EDGE * j : EDGE * j + EDGE, slot].astype(jnp.float32)
        for j in range(2)
    ]
    return jnp.concatenate(pair, axis=1).reshape(EDGE * ROWS, WIDTH)


def add_terms(total, first, part):
    for c in range(3):
        for s in range(2):
            half = 2 * (first + c) + s
            if isinstance(half, int):
                core, start = half // 27, half * 64 - half // 27 * HALF
            else:
                core = (half >= 27).astype(jnp.int32)
                start = pl.multiple_of(half * 64 - core * HALF, 64)
            total[core, pl.ds(start, 64)] += part[s * 64 : s * 64 + 64, c * WIDTH : (c + 1) * WIDTH]


def terms_kernel(i, nbr, lz, grad, feat, keep, *refs):
    *before, terms, field, view, own = refs
    fill_field(i, grad, keep, None, field)
    terms[...] = before[0][...] if before else jnp.zeros_like(terms)

    def unit(slot, carry):
        @pl.when(pair_live(lz, i, slot))
        def _():
            fill_view(nbr, field, view, i, slot)

            def own_rows(xl, c2):
                own[xl] = pair_row(feat, keep, EDGE * i + xl, slot).astype(jnp.bfloat16)
                return c2

            lax.fori_loop(0, EDGE, own_rows, 0)
            own_t = own[...].reshape(UNIT, WIDTH).T

            def offset(t, c2):
                part = jnp.dot(own_t, columns_at(view, t), preferred_element_type=jnp.float32)
                add_terms(terms, 3 * t, part)
                return c2

            lax.fori_loop(0, 9, offset, 0)

        return carry

    lax.fori_loop(0, 2, unit, 0)


def edge_kernel(nbr, lz, core, feat, keep, top, bottom, left, right, before, mine, theirs, total, strip, side, row_view, side_view):
    nx, ny = feat.shape[0], feat.shape[1]
    total[...] = before[...]
    for i in range(2):
        spot = (0, nx + 1)[i]
        strip[i, 1 : ny + 1, 0:2] = (top, bottom)[i][0].astype(jnp.float32)
        strip[i, 0, 0:2] = left[spot, 0].astype(jnp.float32)
        strip[i, ny + 1, 0:2] = right[spot, 0].astype(jnp.float32)
        side[i, 1 : nx + 1, 0:2] = (left, right)[i][1 : nx + 1, 0].astype(jnp.float32)
        for end in (0, nx + 1):
            side[i, end, 0:2] = jnp.zeros((2, EDGE, WIDTH), jnp.float32)
    strip[:, :, 2] = jnp.zeros((2, ny + 2, EDGE, WIDTH), jnp.float32)
    side[:, :, 2] = jnp.zeros((2, nx + 2, EDGE, WIDTH), jnp.float32)

    def product(own_t, pieces, first):
        columns = jnp.concatenate(pieces, axis=1).astype(jnp.bfloat16)
        add_terms(total, first, jnp.dot(own_t, columns, preferred_element_type=jnp.float32))

    def unit(i, slot):
        for q, (start, count) in enumerate(REGIONS):
            halves = []
            for j in range(2):
                base = table_base(i, j, slot) + 18 * i + 3 * q
                span = pl.ds(EDGE * j + start, count)
                halves.append(shifted(*(strip[i, span, nbr[base + r]] for r in range(3))))
            for c in range(3):
                both = jnp.concatenate([halves[0][c], halves[1][c]], axis=1)
                row_view[c, start : start + count] = both.astype(jnp.bfloat16)
        own_t = pair_row(feat, keep, (0, nx - 1)[i], slot).T.astype(jnp.bfloat16)
        for b in range(3):
            pieces = [row_view[c, 2 - b : 2 - b + EDGE].reshape(EDGE * ROWS, WIDTH) for c in range(3)]
            product(own_t, pieces, 18 - 18 * i + 3 * b)
        for j in range(2):
            for p, (start, count) in enumerate(REGIONS):
                base = table_base(i, j, slot) + 9 * p + 6 * j
                span = pl.ds(EDGE * i + start, count)
                moved = shifted(*(side[j, span, nbr[base + r]] for r in range(3)))
                for c in range(3):
                    side_view[c, start : start + count] = moved[c]
            spot = (slice(EDGE * i, EDGE * i + EDGE), (0, ny - 1)[j], slot)
            own_t = (feat[spot].astype(jnp.float32) * keep[spot].astype(jnp.float32)).reshape(EDGE * EDGE, WIDTH)
            own_t = own_t.T.astype(jnp.bfloat16)
            for a in range(3):
                pieces = [side_view[c, 2 - a : 2 - a + EDGE].reshape(EDGE * EDGE, WIDTH) for c in range(3)]
                product(own_t, pieces, 9 * a + 6 - 6 * j)

    for i in range(2):

        def slots(slot, carry, i=i):
            @pl.when(pair_live(lz, i, slot))
            def _():
                unit(i, slot)

            return carry

        lax.fori_loop(0, 2, slots, 0)
    here = core[0]
    chunk = theirs.shape[1] - EDGE
    mine[...] = total[here]
    for n in range(theirs.shape[0]):
        encode(total[1 - here, n * chunk : n * chunk + chunk], theirs, (n,))


def feature_kernel(i, nbr, lz, grad, keep, top, bottom, left, right, wrows, *refs):
    out, field, view, acc = refs[-4:]
    ny = grad.shape[1]
    fill_field(i, grad, keep, (top, bottom, left, right), field)

    def unit(slot, carry):
        live = pair_live(lz, i, slot)

        @pl.when(live)
        def _():
            fill_view(nbr, field, view, i, slot)
            acc[...] = jnp.zeros_like(acc)

            def offset(t, c2):
                weights = wrows[pl.ds(pl.multiple_of(t * 3 * WIDTH, 3 * WIDTH), 3 * WIDTH), :]
                acc[...] += jnp.dot(columns_at(view, t), weights, preferred_element_type=jnp.float32)
                return c2

            lax.fori_loop(0, 9, offset, 0)

            def emit(xl, c2):
                x = EDGE * i + xl
                block = acc[pl.ds(pl.multiple_of(xl * EDGE * ROWS, EDGE * ROWS), EDGE * ROWS), :]
                block = block.reshape(EDGE, 2, EDGE, WIDTH)
                for j in range(2):
                    k = keep[x, EDGE * j : EDGE * j + EDGE, slot].astype(jnp.float32)
                    out[xl, EDGE * j : EDGE * j + EDGE, slot] = (block[:, j] * k).astype(jnp.bfloat16)
                return c2

            lax.fori_loop(0, EDGE, emit, 0)

        @pl.when(jnp.logical_not(live))
        def _():
            def blank(xl, c2):
                out[xl, :, slot] = jnp.zeros((ny, EDGE, WIDTH), jnp.bfloat16)
                return c2

            lax.fori_loop(0, EDGE, blank, 0)

        return carry

    lax.fori_loop(0, 2, unit, 0)


def encode(value, coded, places):
    rows = value.shape[0]
    peak = jnp.max(jnp.abs(value), axis=0, keepdims=True)
    power = jnp.floor(jnp.log2(jnp.maximum(peak, 1e-30)) + 1.001)
    code = jnp.clip(jnp.round(value * jnp.exp2(15.0 - power)), -32767.0, 32767.0)
    code = code.astype(jnp.int32).astype(jnp.int16)
    power = jnp.broadcast_to(power, (EDGE, WIDTH)).astype(jnp.int32).astype(jnp.int16)
    for place in places:
        coded[place, 0:rows] = code
        coded[place, rows : rows + EDGE] = power


def decode(coded):
    rows = coded.shape[0] - EDGE
    power = coded[rows:].astype(jnp.int32).astype(jnp.float32)[0:1]
    return coded[:rows].astype(jnp.int32).astype(jnp.float32) * jnp.exp2(power - 15.0)


def encode_half_kernel(mine, theirs, coded):
    chunk = coded.shape[1] - EDGE
    for n in range(coded.shape[0]):
        encode(mine[n * chunk : n * chunk + chunk] + decode(theirs[n]), coded, (n,))


def sum_kernel(scale, coded, again):
    total = decode(coded[0])
    for n in range(1, coded.shape[0]):
        total = total + decode(coded[n])
    encode(total * scale, again, range(again.shape[0]))


def decode_kernel(core, mine, theirs, out):
    chunk = mine.shape[1] - EDGE
    here = core[0]
    for base, coded in ((here * HALF, mine), ((1 - here) * HALF, theirs)):
        for n in range(coded.shape[0]):
            rows = min(chunk, HALF - n * chunk)
            out[pl.ds(pl.multiple_of(base + n * chunk, EDGE), rows)] = decode(coded[n])[0:rows]


SMEM = pl.BlockSpec(memory_space=pltpu.SMEM)
VMEM = pl.BlockSpec(memory_space=pltpu.VMEM)


def call(kernel, name, out_shape, scratch=(), scalars=0, flops=0, nbytes=4 << 20):
    def run(*args):
        return pl.pallas_call(
            kernel,
            out_shape=out_shape,
            in_specs=[SMEM] * scalars + [VMEM] * (len(args) - scalars),
            out_specs=jax.tree.map(lambda _: VMEM, out_shape),
            scratch_shapes=list(scratch),
            compiler_params=pltpu.CompilerParams(vmem_limit_bytes=40 << 20),
            cost_estimate=pl.CostEstimate(flops=flops, bytes_accessed=nbytes, transcendentals=0),
            name=name,
        )(*args)

    return run


def features_call(i, args, scratch, flops, before=None):
    grad = args[2]
    block = (EDGE,) + grad.shape[1:]
    specs = [SMEM, SMEM] + [VMEM] * (len(args) - 2)
    if before is not None:
        args = args + (before,)
        specs.append(pl.BlockSpec(memory_space=pl.ANY))
    return pl.pallas_call(
        lambda *refs: feature_kernel(i, *refs),
        grid=(1,),
        out_shape=jax.ShapeDtypeStruct(grad.shape, jnp.bfloat16),
        in_specs=specs,
        out_specs=pl.BlockSpec(block, lambda g: (i, 0, 0, 0, 0)),
        scratch_shapes=list(scratch),
        input_output_aliases={} if before is None else {len(args) - 1: 0},
        compiler_params=pltpu.CompilerParams(vmem_limit_bytes=40 << 20),
        cost_estimate=pl.CostEstimate(flops=flops, bytes_accessed=4 << 20, transcendentals=0),
        name="conv_features",
    )(*args)


def exchange(blocks, axis):
    return lax.all_to_all(blocks, axis, 0, 0)


def local(features, grad_out, occupancy, leaf_z, neighbours, kernel):
    nx, ny = grad_out.shape[1], grad_out.shape[2]
    grad = grad_out[0]
    feat = features[0]
    active = (leaf_z[0] >= 0).astype(jnp.int32)
    active_vox = jnp.repeat(jnp.repeat(active, EDGE, axis=0), EDGE, axis=1)
    keep = (occupancy[0] * active_vox[..., None]).astype(jnp.bfloat16)
    keep = jnp.broadcast_to(keep[..., None], grad.shape)
    nbr = neighbours.reshape(-1)
    lz = leaf_z.reshape(-1)
    gx, gy = lax.axis_size("gx"), lax.axis_size("gy")
    core = lax.axis_index("dcn").astype(jnp.int32).reshape(1)
    scale = 1.0 / math.sqrt(lax.axis_size("dcn") * gx * gy * nx * ny * 2 * EDGE)
    field = pltpu.VMEM((VIEW, ny + 2, 3, EDGE, WIDTH), jnp.float32)
    view = pltpu.VMEM((3, VIEW, VIEW, ROWS, WIDTH), jnp.bfloat16)
    own = pltpu.VMEM((EDGE, EDGE * ROWS, WIDTH), jnp.bfloat16)
    acc = pltpu.VMEM((UNIT, WIDTH), jnp.float32)
    terms_shape = jax.ShapeDtypeStruct((2, PADDED, WIDTH), jnp.float32)
    product = 2 * 2 * 512 * 27 * WIDTH * WIDTH

    def shift(block, axis, step):
        count = lax.axis_size(axis)
        pairs = [(i, i + step) for i in range(count) if 0 <= i + step < count]
        return lax.ppermute(block, axis, pairs)

    def terms_of(i, *before):
        return call(
            lambda *refs: terms_kernel(i, *refs),
            "conv_terms",
            terms_shape,
            (field, view, own),
            scalars=2,
            flops=product,
        )(nbr, lz, grad, feat, keep, *before)

    def coded(count):
        return jax.ShapeDtypeStruct((count, PADDED // gy + EDGE, WIDTH), jnp.int16)

    top = shift(grad[nx - 1 :] * keep[nx - 1 :], "gx", 1)
    bottom = shift(grad[:1] * keep[:1], "gx", -1)
    terms = terms_of(0)
    top, bottom, terms = lax.optimization_barrier((top, bottom, terms))

    def side(y):
        return jnp.concatenate(
            [top[:, y : y + 1], grad[:, y : y + 1] * keep[:, y : y + 1], bottom[:, y : y + 1]], axis=0
        )

    left = shift(side(ny - 1), "gy", 1)
    right = shift(side(0), "gy", -1)
    terms = terms_of(1, terms)
    wrows = jnp.transpose(kernel, (0, 2, 1)).reshape(27 * WIDTH, WIDTH)
    edges = (top, bottom, left, right)
    mine, theirs = call(
        edge_kernel,
        "edge_terms",
        (jax.ShapeDtypeStruct((PADDED, WIDTH), jnp.float32), coded(gy)),
        (
            pltpu.VMEM((2, PADDED, WIDTH), jnp.float32),
            pltpu.VMEM((2, ny + 2, 3, EDGE, WIDTH), jnp.float32),
            pltpu.VMEM((2, nx + 2, 3, EDGE, WIDTH), jnp.float32),
            pltpu.VMEM((3, VIEW, ROWS, WIDTH), jnp.bfloat16),
            pltpu.VMEM((3, VIEW, EDGE, WIDTH), jnp.float32),
        ),
        scalars=3,
        flops=product // 4,
    )(nbr, lz, core, feat, keep, *edges, terms)
    theirs = lax.ppermute(theirs, "dcn", [(0, 1), (1, 0)])
    half = call(encode_half_kernel, "encode_half", coded(gy), nbytes=2 << 20)(mine, theirs)

    grad_late, half = lax.optimization_barrier((grad, half))
    out = features_call(0, (nbr, lz, grad_late, keep) + edges + (wrows,), (field, view, acc), product)
    half = exchange(half, "gy")
    piece = call(lambda c, o: sum_kernel(1.0, c, o), "sum_piece", coded(gx), nbytes=1 << 20)(half)
    piece, out = lax.optimization_barrier((piece, out))
    piece = exchange(piece, "gx")
    total = call(lambda c, o: sum_kernel(scale, c, o), "sum_total", coded(gy), nbytes=1 << 20)(piece)
    grad_last, total = lax.optimization_barrier((grad_late, total))
    out = features_call(1, (nbr, lz, grad_last, keep) + edges + (wrows,), (field, view, acc), product, out)
    total, out = lax.optimization_barrier((exchange(total, "gy"), out))
    other = lax.ppermute(total, "dcn", [(0, 1), (1, 0)])
    kernel_grad = call(
        decode_kernel,
        "decode_total",
        jax.ShapeDtypeStruct((27 * WIDTH, WIDTH), jnp.float32),
        scalars=1,
        nbytes=3 << 20,
    )(core, total, other)
    return out[None], kernel_grad.reshape(27, WIDTH, WIDTH)


def solution(mesh):
    return jax.shard_map(
        local,
        mesh=mesh,
        in_specs=(
            P("dcn", "gx", "gy", None, None, None),
            P("dcn", "gx", "gy", None, None, None),
            P("dcn", "gx", "gy", None, None),
            P("dcn", "gx", "gy", None),
            P("dcn", "gx", "gy", None, None),
            P(),
        ),
        out_specs=(P("dcn", "gx", "gy", None, None, None), P()),
        check_vma=False,
    )
```

```python
import math

import jax
import jax.numpy as jnp
from jax import lax
from jax.experimental import pallas as pl
from jax.experimental.pallas import tpu as pltpu
from jax.sharding import PartitionSpec as P

EDGE = 8
WIDTH = 128
VIEW = EDGE + 2
ROWS = 2 * EDGE
UNIT = EDGE * EDGE * ROWS
HALF = 27 * WIDTH // 2
PADDED = 1792


def shifted(below, here, above):
    row = lax.broadcasted_iota(jnp.int32, here.shape, 1)
    return (
        pltpu.roll(jnp.where(row == 0, above, here), EDGE - 1, 1),
        here,
        pltpu.roll(jnp.where(row == EDGE - 1, below, here), 1, 1),
    )


REGIONS = ((0, 1), (1, EDGE), (EDGE + 1, 1))


def slots_of(nbr, i, j, slot, first):
    return [nbr[0, i, j, slot, first + r] for r in range(3)]


def live_at(lz, i, j, slot):
    return lz[0, i, j, slot] >= 0


def pair_live(lz, i, slot):
    return jnp.logical_or(live_at(lz, i, 0, slot), live_at(lz, i, 1, slot))


def kept(value, keep, live):
    return value.astype(jnp.float32) * (keep.astype(jnp.float32) * live.astype(jnp.float32))


def fill_field(i, grad, keep, halo, field):
    nx, ny = grad.shape[0], grad.shape[1]
    low, high = (1, VIEW) if i == 0 else (0, VIEW - 1)

    def fill(r, carry):
        x = EDGE * i - 1 + r
        field[r, 1 : ny + 1, 0:2] = grad[x].astype(jnp.float32) * keep[x].astype(jnp.float32)
        return carry

    lax.fori_loop(low, high, fill, 0)
    outer = 0 if i == 0 else VIEW - 1
    field[:, :, 2] = jnp.zeros((VIEW, ny + 2, EDGE, WIDTH), jnp.float32)
    if halo is None:
        field[outer, :, 0:2] = jnp.zeros((ny + 2, 2, EDGE, WIDTH), jnp.float32)
        field[:, 0, 0:2] = jnp.zeros((VIEW, 2, EDGE, WIDTH), jnp.float32)
        field[:, ny + 1, 0:2] = jnp.zeros((VIEW, 2, EDGE, WIDTH), jnp.float32)
    else:
        left = 2 * ny + EDGE * i
        right = left + nx + 2
        field[outer, 1 : ny + 1, 0:2] = halo[ny * i : ny * i + ny].astype(jnp.float32)
        field[:, 0, 0:2] = halo[left : left + VIEW].astype(jnp.float32)
        field[:, ny + 1, 0:2] = halo[right : right + VIEW].astype(jnp.float32)


def fill_view(nbr, field, view, i, slot):
    def view_rows(xl, p):
        for q, (start, count) in enumerate(REGIONS):
            halves = []
            for j in range(2):
                span = pl.ds(EDGE * j + start, count)
                halves.append(shifted(*(field[xl, span, s] for s in slots_of(nbr, i, j, slot, 9 * p + 3 * q))))
            for c in range(3):
                both = jnp.concatenate([halves[0][c], halves[1][c]], axis=1)
                view[c, xl, start : start + count] = both.astype(jnp.bfloat16)

    view_rows(0, 0)

    def middle(xl, carry):
        view_rows(xl, 1)
        return carry

    lax.fori_loop(1, EDGE + 1, middle, 0)
    view_rows(EDGE + 1, 2)


def columns_at(view, t):
    a = t // 3
    b = t % 3
    pieces = [view[c, pl.ds(2 - a, EDGE), pl.ds(2 - b, EDGE)].reshape(UNIT, WIDTH) for c in range(3)]
    return jnp.concatenate(pieces, axis=1)


def pair_row(lz, feat, keep, i, x, slot):
    pair = []
    for j in range(2):
        spot = (x, slice(EDGE * j, EDGE * j + EDGE), slot)
        pair.append(kept(feat[spot], keep[spot], live_at(lz, i, j, slot)))
    return jnp.concatenate(pair, axis=1).reshape(EDGE * ROWS, WIDTH)


def add_terms(total, first, part):
    for c in range(3):
        for s in range(2):
            half = 2 * (first + c) + s
            if isinstance(half, int):
                core, start = half // 27, half * 64 - half // 27 * HALF
            else:
                core = (half >= 27).astype(jnp.int32)
                start = pl.multiple_of(half * 64 - core * HALF, 64)
            total[core, pl.ds(start, 64)] += part[s * 64 : s * 64 + 64, c * WIDTH : (c + 1) * WIDTH]


def terms_kernel(nbr, lz, grad, feat, keep, terms, field, view, own):
    terms[...] = jnp.zeros_like(terms)
    for i in range(2):
        fill_field(i, grad, keep, None, field)

        def unit(slot, carry, i=i):
            @pl.when(pair_live(lz, i, slot))
            def _():
                fill_view(nbr, field, view, i, slot)

                def own_rows(xl, c2):
                    own[xl] = pair_row(lz, feat, keep, i, EDGE * i + xl, slot).astype(jnp.bfloat16)
                    return c2

                lax.fori_loop(0, EDGE, own_rows, 0)
                own_t = own[...].reshape(UNIT, WIDTH).T

                def offset(t, c2):
                    part = jnp.dot(own_t, columns_at(view, t), preferred_element_type=jnp.float32)
                    add_terms(terms, 3 * t, part)
                    return c2

                lax.fori_loop(0, 9, offset, 0)

            return carry

        lax.fori_loop(0, 2, unit, 0)


def edge_kernel(nbr, lz, core, feat, keep, top, bottom, left, right, before, mine, theirs, halo, total, strip, side, row_view, side_view):
    nx, ny = feat.shape[0], feat.shape[1]
    total[...] = before[...]
    halo[0:ny] = top[0]
    halo[ny : 2 * ny] = bottom[0]
    halo[2 * ny : 2 * ny + nx + 2] = left[:, 0]
    halo[2 * ny + nx + 2 :] = right[:, 0]
    for i in range(2):
        spot = (0, nx + 1)[i]
        strip[i, 1 : ny + 1, 0:2] = (top, bottom)[i][0].astype(jnp.float32)
        strip[i, 0, 0:2] = left[spot, 0].astype(jnp.float32)
        strip[i, ny + 1, 0:2] = right[spot, 0].astype(jnp.float32)
        side[i, 1 : nx + 1, 0:2] = (left, right)[i][1 : nx + 1, 0].astype(jnp.float32)
        for end in (0, nx + 1):
            side[i, end, 0:2] = jnp.zeros((2, EDGE, WIDTH), jnp.float32)
    strip[:, :, 2] = jnp.zeros((2, ny + 2, EDGE, WIDTH), jnp.float32)
    side[:, :, 2] = jnp.zeros((2, nx + 2, EDGE, WIDTH), jnp.float32)

    def product(own_t, pieces, first):
        columns = jnp.concatenate(pieces, axis=1).astype(jnp.bfloat16)
        add_terms(total, first, jnp.dot(own_t, columns, preferred_element_type=jnp.float32))

    def unit(i, slot):
        for q, (start, count) in enumerate(REGIONS):
            halves = []
            for j in range(2):
                span = pl.ds(EDGE * j + start, count)
                halves.append(shifted(*(strip[i, span, s] for s in slots_of(nbr, i, j, slot, 18 * i + 3 * q))))
            for c in range(3):
                both = jnp.concatenate([halves[0][c], halves[1][c]], axis=1)
                row_view[c, start : start + count] = both.astype(jnp.bfloat16)
        own_t = pair_row(lz, feat, keep, i, (0, nx - 1)[i], slot).T.astype(jnp.bfloat16)
        for b in range(3):
            pieces = [row_view[c, 2 - b : 2 - b + EDGE].reshape(EDGE * ROWS, WIDTH) for c in range(3)]
            product(own_t, pieces, 18 - 18 * i + 3 * b)
        for j in range(2):
            for p, (start, count) in enumerate(REGIONS):
                span = pl.ds(EDGE * i + start, count)
                moved = shifted(*(side[j, span, s] for s in slots_of(nbr, i, j, slot, 9 * p + 6 * j)))
                for c in range(3):
                    side_view[c, start : start + count] = moved[c]
            spot = (slice(EDGE * i, EDGE * i + EDGE), (0, ny - 1)[j], slot)
            own_t = kept(feat[spot], keep[spot], live_at(lz, i, j, slot)).reshape(EDGE * EDGE, WIDTH)
            own_t = own_t.T.astype(jnp.bfloat16)
            for a in range(3):
                pieces = [side_view[c, 2 - a : 2 - a + EDGE].reshape(EDGE * EDGE, WIDTH) for c in range(3)]
                product(own_t, pieces, 9 * a + 6 - 6 * j)

    for i in range(2):

        def slots(slot, carry, i=i):
            @pl.when(pair_live(lz, i, slot))
            def _():
                unit(i, slot)

            return carry

        lax.fori_loop(0, 2, slots, 0)
    here = core[0]
    chunk = theirs.shape[1] - EDGE
    mine[...] = total[here]
    for n in range(theirs.shape[0]):
        encode(total[1 - here, n * chunk : n * chunk + chunk], theirs, (n,))


def feature_kernel(i, nbr, lz, grad, keep, halo, wrows, *refs):
    out, field, view, acc = refs[-4:]
    ny = grad.shape[1]
    fill_field(i, grad, keep, halo, field)

    def unit(slot, carry):
        live = pair_live(lz, i, slot)

        @pl.when(live)
        def _():
            fill_view(nbr, field, view, i, slot)
            acc[...] = jnp.zeros_like(acc)

            def offset(t, c2):
                weights = wrows[pl.ds(pl.multiple_of(t * 3 * WIDTH, 3 * WIDTH), 3 * WIDTH), :]
                acc[...] += jnp.dot(columns_at(view, t), weights, preferred_element_type=jnp.float32)
                return c2

            lax.fori_loop(0, 9, offset, 0)

            def emit(xl, c2):
                x = EDGE * i + xl
                block = acc[pl.ds(pl.multiple_of(xl * EDGE * ROWS, EDGE * ROWS), EDGE * ROWS), :]
                block = block.reshape(EDGE, 2, EDGE, WIDTH)
                for j in range(2):
                    span = slice(EDGE * j, EDGE * j + EDGE)
                    value = kept(block[:, j], keep[x, span, slot], live_at(lz, i, j, slot))
                    out[xl, span, slot] = value.astype(jnp.bfloat16)
                return c2

            lax.fori_loop(0, EDGE, emit, 0)

        @pl.when(jnp.logical_not(live))
        def _():
            def blank(xl, c2):
                out[xl, :, slot] = jnp.zeros((ny, EDGE, WIDTH), jnp.bfloat16)
                return c2

            lax.fori_loop(0, EDGE, blank, 0)

        return carry

    lax.fori_loop(0, 2, unit, 0)


def encode(value, coded, places):
    rows = value.shape[0]
    peak = jnp.max(jnp.abs(value), axis=0, keepdims=True)
    power = jnp.floor(jnp.log2(jnp.maximum(peak, 1e-30)) + 1.001)
    code = jnp.clip(jnp.round(value * jnp.exp2(15.0 - power)), -32767.0, 32767.0)
    code = code.astype(jnp.int32).astype(jnp.int16)
    power = jnp.broadcast_to(power, (EDGE, WIDTH)).astype(jnp.int32).astype(jnp.int16)
    for place in places:
        coded[place, 0:rows] = code
        coded[place, rows : rows + EDGE] = power


def decode(coded):
    rows = coded.shape[0] - EDGE
    power = coded[rows:].astype(jnp.int32).astype(jnp.float32)[0:1]
    return coded[:rows].astype(jnp.int32).astype(jnp.float32) * jnp.exp2(power - 15.0)


def encode_half_kernel(mine, theirs, coded):
    chunk = coded.shape[1] - EDGE
    for n in range(coded.shape[0]):
        encode(mine[n * chunk : n * chunk + chunk] + decode(theirs[n]), coded, (n,))


def sum_kernel(scale, coded, again):
    total = decode(coded[0])
    for n in range(1, coded.shape[0]):
        total = total + decode(coded[n])
    encode(total * scale, again, range(again.shape[0]))


def decode_kernel(core, mine, theirs, out):
    chunk = mine.shape[1] - EDGE
    here = core[0]
    for base, coded in ((here * HALF, mine), ((1 - here) * HALF, theirs)):
        for n in range(coded.shape[0]):
            rows = min(chunk, HALF - n * chunk)
            out[pl.ds(pl.multiple_of(base + n * chunk, EDGE), rows)] = decode(coded[n])[0:rows]


SMEM = pl.BlockSpec(memory_space=pltpu.SMEM)
VMEM = pl.BlockSpec(memory_space=pltpu.VMEM)


def call(kernel, name, out_shape, scratch=(), scalars=0, flops=0, nbytes=4 << 20):
    def run(*args):
        return pl.pallas_call(
            kernel,
            out_shape=out_shape,
            in_specs=[SMEM] * scalars + [VMEM] * (len(args) - scalars),
            out_specs=jax.tree.map(lambda _: VMEM, out_shape),
            scratch_shapes=list(scratch),
            compiler_params=pltpu.CompilerParams(vmem_limit_bytes=20 << 20),
            cost_estimate=pl.CostEstimate(flops=flops, bytes_accessed=nbytes, transcendentals=0),
            name=name,
        )(*args)

    return run


def features_call(i, args, scratch, flops, before=None):
    grad = args[2]
    block = (EDGE,) + grad.shape[1:]
    specs = [SMEM, SMEM] + [VMEM] * (len(args) - 2)
    if before is not None:
        args = args + (before,)
        specs.append(pl.BlockSpec(memory_space=pl.ANY))
    return pl.pallas_call(
        lambda *refs: feature_kernel(i, *refs),
        grid=(1,),
        out_shape=jax.ShapeDtypeStruct(grad.shape, jnp.bfloat16),
        in_specs=specs,
        out_specs=pl.BlockSpec(block, lambda g: (i, 0, 0, 0, 0)),
        scratch_shapes=list(scratch),
        input_output_aliases={} if before is None else {len(args) - 1: 0},
        compiler_params=pltpu.CompilerParams(vmem_limit_bytes=20 << 20),
        cost_estimate=pl.CostEstimate(flops=flops, bytes_accessed=4 << 20, transcendentals=0),
        name="conv_features",
    )(*args)


def exchange(blocks, axis):
    return lax.all_to_all(blocks, axis, 0, 0)


def local(features, grad_out, occupancy, leaf_z, neighbours, kernel):
    nx, ny = grad_out.shape[1], grad_out.shape[2]
    grad = grad_out[0]
    feat = features[0]
    keep = jnp.broadcast_to(occupancy[0].astype(jnp.bfloat16)[..., None], grad.shape)
    gx, gy = lax.axis_size("gx"), lax.axis_size("gy")
    core = lax.axis_index("dcn").astype(jnp.int32).reshape(1)
    scale = 1.0 / math.sqrt(lax.axis_size("dcn") * gx * gy * nx * ny * 2 * EDGE)
    field = pltpu.VMEM((VIEW, ny + 2, 3, EDGE, WIDTH), jnp.float32)
    view = pltpu.VMEM((3, VIEW, VIEW, ROWS, WIDTH), jnp.bfloat16)
    own = pltpu.VMEM((EDGE, EDGE * ROWS, WIDTH), jnp.bfloat16)
    acc = pltpu.VMEM((UNIT, WIDTH), jnp.float32)
    product = 2 * 2 * 512 * 27 * WIDTH * WIDTH

    def shift(block, axis, step):
        count = lax.axis_size(axis)
        pairs = [(i, i + step) for i in range(count) if 0 <= i + step < count]
        return lax.ppermute(block, axis, pairs)

    def coded(count):
        return jax.ShapeDtypeStruct((count, PADDED // gy + EDGE, WIDTH), jnp.int16)

    core, last = lax.optimization_barrier((core, grad[nx - 1 :] * keep[nx - 1 :]))
    top = shift(last, "gx", 1)
    bottom = shift(grad[:1] * keep[:1], "gx", -1)

    def side(y):
        return jnp.concatenate(
            [top[:, y : y + 1], grad[:, y : y + 1] * keep[:, y : y + 1], bottom[:, y : y + 1]], axis=0
        )

    left = shift(side(ny - 1), "gy", 1)
    right = shift(side(0), "gy", -1)
    terms = call(
        terms_kernel,
        "conv_terms",
        jax.ShapeDtypeStruct((2, PADDED, WIDTH), jnp.float32),
        (field, view, own),
        scalars=2,
        flops=2 * product,
    )(neighbours, leaf_z, grad, feat, keep)
    wrows = jnp.transpose(kernel, (0, 2, 1)).reshape(27 * WIDTH, WIDTH)
    edges = (top, bottom, left, right)
    mine, theirs, halo = call(
        edge_kernel,
        "edge_terms",
        (
            jax.ShapeDtypeStruct((PADDED, WIDTH), jnp.float32),
            coded(gy),
            jax.ShapeDtypeStruct((2 * (nx + ny + 2), 2, EDGE, WIDTH), jnp.bfloat16),
        ),
        (
            pltpu.VMEM((2, PADDED, WIDTH), jnp.float32),
            pltpu.VMEM((2, ny + 2, 3, EDGE, WIDTH), jnp.float32),
            pltpu.VMEM((2, nx + 2, 3, EDGE, WIDTH), jnp.float32),
            pltpu.VMEM((3, VIEW, ROWS, WIDTH), jnp.bfloat16),
            pltpu.VMEM((3, VIEW, EDGE, WIDTH), jnp.float32),
        ),
        scalars=3,
        flops=product // 4,
    )(neighbours, leaf_z, core, feat, keep, *edges, terms)
    theirs = lax.ppermute(theirs, "dcn", [(0, 1), (1, 0)])
    half = call(encode_half_kernel, "encode_half", coded(gy), nbytes=2 << 20)(mine, theirs)

    def features_part(i, value, *before):
        late, value = lax.optimization_barrier((grad, value))
        args = (neighbours, leaf_z, late, keep, halo, wrows)
        return features_call(i, args, (field, view, acc), product, *before), value

    half = exchange(half, "gy")
    piece = call(lambda c, o: sum_kernel(1.0, c, o), "sum_piece", coded(gx), nbytes=1 << 20)(half)
    out, piece = features_part(0, piece)
    piece, out = lax.optimization_barrier((exchange(piece, "gx"), out))
    total = call(lambda c, o: sum_kernel(scale, c, o), "sum_total", coded(gy), nbytes=1 << 20)(piece)
    out, total = features_part(1, total, out)
    total, out = lax.optimization_barrier((exchange(total, "gy"), out))
    other = lax.ppermute(total, "dcn", [(0, 1), (1, 0)])
    kernel_grad = call(
        decode_kernel,
        "decode_total",
        jax.ShapeDtypeStruct((27 * WIDTH, WIDTH), jnp.float32),
        scalars=1,
        nbytes=3 << 20,
    )(core, total, other)
    return out[None], kernel_grad.reshape(27, WIDTH, WIDTH)


def solution(mesh):
    return jax.shard_map(
        local,
        mesh=mesh,
        in_specs=(
            P("dcn", "gx", "gy", None, None, None),
            P("dcn", "gx", "gy", None, None, None),
            P("dcn", "gx", "gy", None, None),
            P("dcn", "gx", "gy", None),
            P("dcn", "gx", "gy", None, None),
            P(),
        ),
        out_specs=(P("dcn", "gx", "gy", None, None, None), P()),
        check_vma=False,
    )
```

```python
import math

import jax
import jax.numpy as jnp
from jax import lax
from jax.experimental import pallas as pl
from jax.experimental.pallas import tpu as pltpu
from jax.sharding import PartitionSpec as P

EDGE = 8
WIDTH = 128
VIEW = EDGE + 2
ROWS = 2 * EDGE
UNIT = EDGE * EDGE * ROWS
HALF = 27 * WIDTH // 2
PADDED = 1792


def shifted(below, here, above):
    row = lax.broadcasted_iota(jnp.int32, here.shape, 1)
    return (
        pltpu.roll(jnp.where(row == 0, above, here), EDGE - 1, 1),
        here,
        pltpu.roll(jnp.where(row == EDGE - 1, below, here), 1, 1),
    )


REGIONS = ((0, 1), (1, EDGE), (EDGE + 1, 1))


def slots_of(nbr, i, j, slot, first):
    return [nbr[0, i, j, slot, first + r] for r in range(3)]


def live_at(lz, i, j, slot):
    return lz[0, i, j, slot] >= 0


def pair_live(lz, i, slot):
    return jnp.logical_or(live_at(lz, i, 0, slot), live_at(lz, i, 1, slot))


def kept(value, keep, live):
    return value.astype(jnp.float32) * (keep.astype(jnp.float32) * live.astype(jnp.float32))


def fill_field(i, grad, keep, halo, field):
    nx, ny = grad.shape[0], grad.shape[1]
    low, high = (1, VIEW) if i == 0 else (0, VIEW - 1)

    def fill(r, carry):
        x = EDGE * i - 1 + r
        field[r, 1 : ny + 1, 0:2] = grad[x].astype(jnp.float32) * keep[x].astype(jnp.float32)
        return carry

    lax.fori_loop(low, high, fill, 0)
    outer = 0 if i == 0 else VIEW - 1
    field[:, :, 2] = jnp.zeros((VIEW, ny + 2, EDGE, WIDTH), jnp.float32)
    if halo is None:
        field[outer, :, 0:2] = jnp.zeros((ny + 2, 2, EDGE, WIDTH), jnp.float32)
        field[:, 0, 0:2] = jnp.zeros((VIEW, 2, EDGE, WIDTH), jnp.float32)
        field[:, ny + 1, 0:2] = jnp.zeros((VIEW, 2, EDGE, WIDTH), jnp.float32)
    else:
        left = 2 * ny + EDGE * i
        right = left + nx + 2
        field[outer, 1 : ny + 1, 0:2] = halo[ny * i : ny * i + ny].astype(jnp.float32)
        field[:, 0, 0:2] = halo[left : left + VIEW].astype(jnp.float32)
        field[:, ny + 1, 0:2] = halo[right : right + VIEW].astype(jnp.float32)


def fill_view(nbr, field, view, i, slot):
    def view_rows(xl, p):
        for q, (start, count) in enumerate(REGIONS):
            halves = []
            for j in range(2):
                span = pl.ds(EDGE * j + start, count)
                halves.append(shifted(*(field[xl, span, s] for s in slots_of(nbr, i, j, slot, 9 * p + 3 * q))))
            for c in range(3):
                both = jnp.concatenate([halves[0][c], halves[1][c]], axis=1)
                view[c, xl, start : start + count] = both.astype(jnp.bfloat16)

    view_rows(0, 0)

    def middle(xl, carry):
        view_rows(xl, 1)
        return carry

    lax.fori_loop(1, EDGE + 1, middle, 0)
    view_rows(EDGE + 1, 2)


def columns_of(view):
    pieces = [
        view[c, 2 - a : 2 - a + EDGE, 2 - b : 2 - b + EDGE].reshape(UNIT, WIDTH)
        for a in range(3)
        for b in range(3)
        for c in range(3)
    ]
    return jnp.concatenate(pieces, axis=1)


def pair_row(lz, feat, keep, i, x, slot):
    pair = []
    for j in range(2):
        spot = (x, slice(EDGE * j, EDGE * j + EDGE), slot)
        pair.append(kept(feat[spot], keep[spot], live_at(lz, i, j, slot)))
    return jnp.concatenate(pair, axis=1).reshape(EDGE * ROWS, WIDTH)


def add_terms(total, first, part):
    for c in range(3):
        for s in range(2):
            half = 2 * (first + c) + s
            core, start = half // 27, half * 64 - half // 27 * HALF
            total[core, start : start + 64] += part[s * 64 : s * 64 + 64, c * WIDTH : (c + 1) * WIDTH]


def terms_kernel(nbr, lz, grad, feat, keep, terms, field, view, own):
    terms[...] = jnp.zeros_like(terms)
    for i in range(2):
        fill_field(i, grad, keep, None, field)

        def unit(slot, carry, i=i):
            @pl.when(pair_live(lz, i, slot))
            def _():
                fill_view(nbr, field, view, i, slot)

                def own_rows(xl, c2):
                    own[xl] = pair_row(lz, feat, keep, i, EDGE * i + xl, slot).astype(jnp.bfloat16)
                    return c2

                lax.fori_loop(0, EDGE, own_rows, 0)
                own_t = own[...].reshape(UNIT, WIDTH).T

                part = jnp.dot(own_t, columns_of(view), preferred_element_type=jnp.float32)
                for k in range(0, 27, 3):
                    add_terms(terms, k, part[:, k * WIDTH : (k + 3) * WIDTH])

            return carry

        lax.fori_loop(0, 2, unit, 0)


def edge_kernel(nbr, lz, core, feat, keep, top, bottom, left, right, before, mine, theirs, halo, total, strip, side, row_view, side_view):
    nx, ny = feat.shape[0], feat.shape[1]
    total[...] = before[...]
    halo[0:ny] = top[0]
    halo[ny : 2 * ny] = bottom[0]
    halo[2 * ny : 2 * ny + nx + 2] = left[:, 0]
    halo[2 * ny + nx + 2 :] = right[:, 0]
    for i in range(2):
        spot = (0, nx + 1)[i]
        strip[i, 1 : ny + 1, 0:2] = (top, bottom)[i][0].astype(jnp.float32)
        strip[i, 0, 0:2] = left[spot, 0].astype(jnp.float32)
        strip[i, ny + 1, 0:2] = right[spot, 0].astype(jnp.float32)
        side[i, 1 : nx + 1, 0:2] = (left, right)[i][1 : nx + 1, 0].astype(jnp.float32)
        for end in (0, nx + 1):
            side[i, end, 0:2] = jnp.zeros((2, EDGE, WIDTH), jnp.float32)
    strip[:, :, 2] = jnp.zeros((2, ny + 2, EDGE, WIDTH), jnp.float32)
    side[:, :, 2] = jnp.zeros((2, nx + 2, EDGE, WIDTH), jnp.float32)

    def product(own_t, pieces, first):
        columns = jnp.concatenate(pieces, axis=1).astype(jnp.bfloat16)
        add_terms(total, first, jnp.dot(own_t, columns, preferred_element_type=jnp.float32))

    def unit(i, slot):
        for q, (start, count) in enumerate(REGIONS):
            halves = []
            for j in range(2):
                span = pl.ds(EDGE * j + start, count)
                halves.append(shifted(*(strip[i, span, s] for s in slots_of(nbr, i, j, slot, 18 * i + 3 * q))))
            for c in range(3):
                both = jnp.concatenate([halves[0][c], halves[1][c]], axis=1)
                row_view[c, start : start + count] = both.astype(jnp.bfloat16)
        own_t = pair_row(lz, feat, keep, i, (0, nx - 1)[i], slot).T.astype(jnp.bfloat16)
        for b in range(3):
            pieces = [row_view[c, 2 - b : 2 - b + EDGE].reshape(EDGE * ROWS, WIDTH) for c in range(3)]
            product(own_t, pieces, 18 - 18 * i + 3 * b)
        for j in range(2):
            for p, (start, count) in enumerate(REGIONS):
                span = pl.ds(EDGE * i + start, count)
                moved = shifted(*(side[j, span, s] for s in slots_of(nbr, i, j, slot, 9 * p + 6 * j)))
                for c in range(3):
                    side_view[c, start : start + count] = moved[c]
            spot = (slice(EDGE * i, EDGE * i + EDGE), (0, ny - 1)[j], slot)
            own_t = kept(feat[spot], keep[spot], live_at(lz, i, j, slot)).reshape(EDGE * EDGE, WIDTH)
            own_t = own_t.T.astype(jnp.bfloat16)
            for a in range(3):
                pieces = [side_view[c, 2 - a : 2 - a + EDGE].reshape(EDGE * EDGE, WIDTH) for c in range(3)]
                product(own_t, pieces, 9 * a + 6 - 6 * j)

    for i in range(2):

        def slots(slot, carry, i=i):
            @pl.when(pair_live(lz, i, slot))
            def _():
                unit(i, slot)

            return carry

        lax.fori_loop(0, 2, slots, 0)
    here = core[0]
    chunk = theirs.shape[1] - EDGE
    mine[...] = total[here]
    for n in range(theirs.shape[0]):
        encode(total[1 - here, n * chunk : n * chunk + chunk], theirs, (n,))


def feature_kernel(i, nbr, lz, grad, keep, halo, kernel, *refs):
    out, field, view, acc = refs[-4:]
    ny = grad.shape[1]
    fill_field(i, grad, keep, halo, field)

    def unit(slot, carry):
        live = pair_live(lz, i, slot)

        @pl.when(live)
        def _():
            fill_view(nbr, field, view, i, slot)
            weights = jnp.concatenate([kernel[k] for k in range(27)], axis=1)
            acc[...] = lax.dot_general(
                columns_of(view), weights, (((1,), (1,)), ((), ())), preferred_element_type=jnp.float32
            )

            def emit(xl, c2):
                x = EDGE * i + xl
                block = acc[pl.ds(pl.multiple_of(xl * EDGE * ROWS, EDGE * ROWS), EDGE * ROWS), :]
                block = block.reshape(EDGE, 2, EDGE, WIDTH)
                for j in range(2):
                    span = slice(EDGE * j, EDGE * j + EDGE)
                    value = kept(block[:, j], keep[x, span, slot], live_at(lz, i, j, slot))
                    out[xl, span, slot] = value.astype(jnp.bfloat16)
                return c2

            lax.fori_loop(0, EDGE, emit, 0)

        @pl.when(jnp.logical_not(live))
        def _():
            def blank(xl, c2):
                out[xl, :, slot] = jnp.zeros((ny, EDGE, WIDTH), jnp.bfloat16)
                return c2

            lax.fori_loop(0, EDGE, blank, 0)

        return carry

    lax.fori_loop(0, 2, unit, 0)


def encode(value, coded, places):
    rows = value.shape[0]
    peak = jnp.max(jnp.abs(value), axis=0, keepdims=True)
    power = jnp.floor(jnp.log2(jnp.maximum(peak, 1e-30)) + 1.001)
    code = jnp.clip(jnp.round(value * jnp.exp2(15.0 - power)), -32767.0, 32767.0)
    code = code.astype(jnp.int32).astype(jnp.int16)
    power = jnp.broadcast_to(power, (EDGE, WIDTH)).astype(jnp.int32).astype(jnp.int16)
    for place in places:
        coded[place, 0:rows] = code
        coded[place, rows : rows + EDGE] = power


def decode(coded):
    rows = coded.shape[0] - EDGE
    power = coded[rows:].astype(jnp.int32).astype(jnp.float32)[0:1]
    return coded[:rows].astype(jnp.int32).astype(jnp.float32) * jnp.exp2(power - 15.0)


def encode_half_kernel(mine, theirs, coded):
    chunk = coded.shape[1] - EDGE
    for n in range(coded.shape[0]):
        encode(mine[n * chunk : n * chunk + chunk] + decode(theirs[n]), coded, (n,))


def sum_kernel(scale, coded, again):
    total = decode(coded[0])
    for n in range(1, coded.shape[0]):
        total = total + decode(coded[n])
    encode(total * scale, again, range(again.shape[0]))


def decode_kernel(core, mine, theirs, out):
    chunk = mine.shape[1] - EDGE
    here = core[0]
    for base, coded in ((here * HALF, mine), ((1 - here) * HALF, theirs)):
        for n in range(coded.shape[0]):
            rows = min(chunk, HALF - n * chunk)
            out[pl.ds(pl.multiple_of(base + n * chunk, EDGE), rows)] = decode(coded[n])[0:rows]


SMEM = pl.BlockSpec(memory_space=pltpu.SMEM)
VMEM = pl.BlockSpec(memory_space=pltpu.VMEM)


def call(kernel, name, out_shape, scratch=(), scalars=0, flops=0, nbytes=4 << 20):
    def run(*args):
        return pl.pallas_call(
            kernel,
            out_shape=out_shape,
            in_specs=[SMEM] * scalars + [VMEM] * (len(args) - scalars),
            out_specs=jax.tree.map(lambda _: VMEM, out_shape),
            scratch_shapes=list(scratch),
            compiler_params=pltpu.CompilerParams(vmem_limit_bytes=20 << 20),
            cost_estimate=pl.CostEstimate(flops=flops, bytes_accessed=nbytes, transcendentals=0),
            name=name,
        )(*args)

    return run


def features_call(i, args, scratch, flops, before=None):
    grad = args[2]
    block = (EDGE,) + grad.shape[1:]
    specs = [SMEM, SMEM] + [VMEM] * (len(args) - 2)
    if before is not None:
        args = args + (before,)
        specs.append(pl.BlockSpec(memory_space=pl.ANY))
    return pl.pallas_call(
        lambda *refs: feature_kernel(i, *refs),
        grid=(1,),
        out_shape=jax.ShapeDtypeStruct(grad.shape, jnp.bfloat16),
        in_specs=specs,
        out_specs=pl.BlockSpec(block, lambda g: (i, 0, 0, 0, 0)),
        scratch_shapes=list(scratch),
        input_output_aliases={} if before is None else {len(args) - 1: 0},
        compiler_params=pltpu.CompilerParams(vmem_limit_bytes=20 << 20),
        cost_estimate=pl.CostEstimate(flops=flops, bytes_accessed=4 << 20, transcendentals=0),
        name="conv_features",
    )(*args)


def exchange(blocks, axis):
    return lax.all_to_all(blocks, axis, 0, 0)


def local(features, grad_out, occupancy, leaf_z, neighbours, kernel):
    nx, ny = grad_out.shape[1], grad_out.shape[2]
    grad = grad_out[0]
    feat = features[0]
    keep = jnp.broadcast_to(occupancy[0].astype(jnp.bfloat16)[..., None], grad.shape)
    gx, gy = lax.axis_size("gx"), lax.axis_size("gy")
    core = lax.axis_index("dcn").astype(jnp.int32).reshape(1)
    scale = 1.0 / math.sqrt(lax.axis_size("dcn") * gx * gy * nx * ny * 2 * EDGE)
    field = pltpu.VMEM((VIEW, ny + 2, 3, EDGE, WIDTH), jnp.float32)
    view = pltpu.VMEM((3, VIEW, VIEW, ROWS, WIDTH), jnp.bfloat16)
    own = pltpu.VMEM((EDGE, EDGE * ROWS, WIDTH), jnp.bfloat16)
    acc = pltpu.VMEM((UNIT, WIDTH), jnp.float32)
    product = 2 * 2 * 512 * 27 * WIDTH * WIDTH

    def shift(block, axis, step):
        count = lax.axis_size(axis)
        pairs = [(i, i + step) for i in range(count) if 0 <= i + step < count]
        return lax.ppermute(block, axis, pairs)

    def coded(count):
        return jax.ShapeDtypeStruct((count, PADDED // gy + EDGE, WIDTH), jnp.int16)

    core, last = lax.optimization_barrier((core, grad[nx - 1 :] * keep[nx - 1 :]))
    top = shift(last, "gx", 1)
    bottom = shift(grad[:1] * keep[:1], "gx", -1)
    sides = [grad[:, y : y + 1] * keep[:, y : y + 1] for y in (0, ny - 1)]
    top, bottom, keep, sides = lax.optimization_barrier((top, bottom, keep, sides))

    def side(y, own):
        return jnp.concatenate([top[:, y : y + 1], own, bottom[:, y : y + 1]], axis=0)

    left = shift(side(ny - 1, sides[1]), "gy", 1)
    right = shift(side(0, sides[0]), "gy", -1)
    terms = call(
        terms_kernel,
        "conv_terms",
        jax.ShapeDtypeStruct((2, PADDED, WIDTH), jnp.float32),
        (field, view, own),
        scalars=2,
        flops=2 * product,
    )(neighbours, leaf_z, grad, feat, keep)
    edges = (top, bottom, left, right)
    mine, theirs, halo = call(
        edge_kernel,
        "edge_terms",
        (
            jax.ShapeDtypeStruct((PADDED, WIDTH), jnp.float32),
            coded(gy),
            jax.ShapeDtypeStruct((2 * (nx + ny + 2), 2, EDGE, WIDTH), jnp.bfloat16),
        ),
        (
            pltpu.VMEM((2, PADDED, WIDTH), jnp.float32),
            pltpu.VMEM((2, ny + 2, 3, EDGE, WIDTH), jnp.float32),
            pltpu.VMEM((2, nx + 2, 3, EDGE, WIDTH), jnp.float32),
            pltpu.VMEM((3, VIEW, ROWS, WIDTH), jnp.bfloat16),
            pltpu.VMEM((3, VIEW, EDGE, WIDTH), jnp.float32),
        ),
        scalars=3,
        flops=product // 4,
    )(neighbours, leaf_z, core, feat, keep, *edges, terms)
    theirs = lax.ppermute(theirs, "dcn", [(0, 1), (1, 0)])
    half = call(encode_half_kernel, "encode_half", coded(gy), nbytes=2 << 20)(mine, theirs)

    def features_part(i, value, *before):
        late, value = lax.optimization_barrier((grad, value))
        args = (neighbours, leaf_z, late, keep, halo, kernel)
        return features_call(i, args, (field, view, acc), product, *before), value

    half = exchange(half, "gy")
    piece = call(lambda c, o: sum_kernel(1.0, c, o), "sum_piece", coded(gx), nbytes=1 << 20)(half)
    out, piece = features_part(0, piece)
    piece, out = lax.optimization_barrier((exchange(piece, "gx"), out))
    total = call(lambda c, o: sum_kernel(scale, c, o), "sum_total", coded(gy), nbytes=1 << 20)(piece)
    out, total = features_part(1, total, out)
    total, out = lax.optimization_barrier((exchange(total, "gy"), out))
    other = lax.ppermute(total, "dcn", [(0, 1), (1, 0)])
    kernel_grad = call(
        decode_kernel,
        "decode_total",
        jax.ShapeDtypeStruct((27 * WIDTH, WIDTH), jnp.float32),
        scalars=1,
        nbytes=3 << 20,
    )(core, total, other)
    return out[None], kernel_grad.reshape(27, WIDTH, WIDTH)


def solution(mesh):
    return jax.shard_map(
        local,
        mesh=mesh,
        in_specs=(
            P("dcn", "gx", "gy", None, None, None),
            P("dcn", "gx", "gy", None, None, None),
            P("dcn", "gx", "gy", None, None),
            P("dcn", "gx", "gy", None),
            P("dcn", "gx", "gy", None, None),
            P(),
        ),
        out_specs=(P("dcn", "gx", "gy", None, None, None), P()),
        check_vma=False,
    )
```

```python
import math

import jax
import jax.numpy as jnp
from jax import lax
from jax.experimental import pallas as pl
from jax.experimental.pallas import tpu as pltpu
from jax.sharding import PartitionSpec as P

EDGE = 8
WIDTH = 128
VIEW = EDGE + 2
ROWS = 2 * EDGE
UNIT = EDGE * EDGE * ROWS
HALF = 27 * WIDTH // 2
PADDED = 1792


def shifted(below, here, above):
    row = lax.broadcasted_iota(jnp.int32, here.shape, 1)
    return (
        pltpu.roll(jnp.where(row == 0, above, here), EDGE - 1, 1),
        here,
        pltpu.roll(jnp.where(row == EDGE - 1, below, here), 1, 1),
    )


REGIONS = ((0, 1), (1, EDGE), (EDGE + 1, 1))


def slots_of(nbr, i, j, slot, first):
    return [nbr[0, i, j, slot, first + r] for r in range(3)]


def live_at(lz, i, j, slot):
    return lz[0, i, j, slot] >= 0


def pair_live(lz, i, slot):
    return jnp.logical_or(live_at(lz, i, 0, slot), live_at(lz, i, 1, slot))


def kept(value, mask, live):
    return value.astype(jnp.float32) * (mask * live.astype(jnp.float32))


def mask_of(occ, x, slot, spots):
    tile = occ[x, slot].astype(jnp.float32)
    return [jnp.broadcast_to(tile[:, y : y + 1], (EDGE, WIDTH)) for y in spots]


def pack_kernel(occ, first, last, start, end, top, bottom, left, right):
    nx, ny = occ.shape[0], occ.shape[3]
    for x, source, target in ((0, first, bottom), (nx - 1, last, top)):
        for slot in range(2):
            for y, mask in enumerate(mask_of(occ, x, slot, range(ny))):
                target[0, y, slot] = (source[0, y, slot].astype(jnp.float32) * mask).astype(jnp.bfloat16)
    for x in range(nx):
        for slot in range(2):
            low, high = mask_of(occ, x, slot, (0, ny - 1))
            right[x, 0, slot] = (start[x, 0, slot].astype(jnp.float32) * low).astype(jnp.bfloat16)
            left[x, 0, slot] = (end[x, 0, slot].astype(jnp.float32) * high).astype(jnp.bfloat16)


def sides_kernel(top, bottom, left, right, left_side, right_side):
    nx, ny = left.shape[0], top.shape[1]
    for own, side, y in ((left, left_side, ny - 1), (right, right_side, 0)):
        side[0, 0] = top[0, y]
        side[1 : nx + 1] = own[...]
        side[nx + 1, 0] = bottom[0, y]


def fill_field(i, grad, occ, halo, field, masks):
    nx, ny = grad.shape[0], grad.shape[1]
    low, high = (1, VIEW) if i == 0 else (0, VIEW - 1)

    def fill(r, carry):
        x = EDGE * i - 1 + r
        values = grad[x].astype(jnp.float32)
        for slot in range(2):
            for y, mask in enumerate(mask_of(occ, x, slot, range(ny))):
                masks[r, y, slot] = mask
                field[r, y + 1, slot] = values[y, slot] * mask
        return carry

    lax.fori_loop(low, high, fill, 0)
    outer = 0 if i == 0 else VIEW - 1
    field[:, :, 2] = jnp.zeros((VIEW, ny + 2, EDGE, WIDTH), jnp.float32)
    if halo is None:
        field[outer, :, 0:2] = jnp.zeros((ny + 2, 2, EDGE, WIDTH), jnp.float32)
        field[:, 0, 0:2] = jnp.zeros((VIEW, 2, EDGE, WIDTH), jnp.float32)
        field[:, ny + 1, 0:2] = jnp.zeros((VIEW, 2, EDGE, WIDTH), jnp.float32)
    else:
        left = 2 * ny + EDGE * i
        right = left + nx + 2
        field[outer, 1 : ny + 1, 0:2] = halo[ny * i : ny * i + ny].astype(jnp.float32)
        field[:, 0, 0:2] = halo[left : left + VIEW].astype(jnp.float32)
        field[:, ny + 1, 0:2] = halo[right : right + VIEW].astype(jnp.float32)


def fill_view(nbr, field, view, i, slot):
    def view_rows(xl, p):
        for q, (start, count) in enumerate(REGIONS):
            halves = []
            for j in range(2):
                span = pl.ds(EDGE * j + start, count)
                halves.append(shifted(*(field[xl, span, s] for s in slots_of(nbr, i, j, slot, 9 * p + 3 * q))))
            for c in range(3):
                both = jnp.concatenate([halves[0][c], halves[1][c]], axis=1)
                view[c, xl, start : start + count] = both.astype(jnp.bfloat16)

    view_rows(0, 0)

    def middle(xl, carry):
        view_rows(xl, 1)
        return carry

    lax.fori_loop(1, EDGE + 1, middle, 0)
    view_rows(EDGE + 1, 2)


def columns_of(view):
    pieces = [
        view[c, 2 - a : 2 - a + EDGE, 2 - b : 2 - b + EDGE].reshape(UNIT, WIDTH)
        for a in range(3)
        for b in range(3)
        for c in range(3)
    ]
    return jnp.concatenate(pieces, axis=1)


def pair_row(lz, feat, masks, i, x, slot):
    pair = []
    for j in range(2):
        span = slice(EDGE * j, EDGE * j + EDGE)
        pair.append(kept(feat[x, span, slot], masks[span], live_at(lz, i, j, slot)))
    return jnp.concatenate(pair, axis=1).reshape(EDGE * ROWS, WIDTH)


def add_terms(total, first, part):
    for c in range(3):
        for s in range(2):
            half = 2 * (first + c) + s
            core, start = half // 27, half * 64 - half // 27 * HALF
            total[core, start : start + 64] += part[s * 64 : s * 64 + 64, c * WIDTH : (c + 1) * WIDTH]


def terms_kernel(i, nbr, lz, grad, feat, occ, *refs):
    *before, terms, field, masks, view, own = refs
    terms[...] = before[0][...] if before else jnp.zeros_like(terms)
    fill_field(i, grad, occ, None, field, masks)

    def unit(slot, carry):
        @pl.when(pair_live(lz, i, slot))
        def _():
            fill_view(nbr, field, view, i, slot)

            def own_rows(xl, c2):
                rows = pair_row(lz, feat, masks[xl + 1, :, slot], i, EDGE * i + xl, slot)
                own[xl] = rows.astype(jnp.bfloat16)
                return c2

            lax.fori_loop(0, EDGE, own_rows, 0)
            own_t = own[...].reshape(UNIT, WIDTH).T
            part = jnp.dot(own_t, columns_of(view), preferred_element_type=jnp.float32)
            for k in range(0, 27, 3):
                add_terms(terms, k, part[:, k * WIDTH : (k + 3) * WIDTH])

        return carry

    lax.fori_loop(0, 2, unit, 0)


def edge_kernel(nbr, lz, core, feat, occ, top, bottom, left, right, before, mine, theirs, halo, total, strip, side, row_view, side_view):
    nx, ny = feat.shape[0], feat.shape[1]
    total[...] = before[...]
    halo[0:ny] = top[0]
    halo[ny : 2 * ny] = bottom[0]
    halo[2 * ny : 2 * ny + nx + 2] = left[:, 0]
    halo[2 * ny + nx + 2 :] = right[:, 0]
    for i in range(2):
        spot = (0, nx + 1)[i]
        strip[i, 1 : ny + 1, 0:2] = (top, bottom)[i][0].astype(jnp.float32)
        strip[i, 0, 0:2] = left[spot, 0].astype(jnp.float32)
        strip[i, ny + 1, 0:2] = right[spot, 0].astype(jnp.float32)
        side[i, 1 : nx + 1, 0:2] = (left, right)[i][1 : nx + 1, 0].astype(jnp.float32)
        for end in (0, nx + 1):
            side[i, end, 0:2] = jnp.zeros((2, EDGE, WIDTH), jnp.float32)
    strip[:, :, 2] = jnp.zeros((2, ny + 2, EDGE, WIDTH), jnp.float32)
    side[:, :, 2] = jnp.zeros((2, nx + 2, EDGE, WIDTH), jnp.float32)

    def product(own_t, pieces, first):
        columns = jnp.concatenate(pieces, axis=1).astype(jnp.bfloat16)
        add_terms(total, first, jnp.dot(own_t, columns, preferred_element_type=jnp.float32))

    def unit(i, slot):
        for q, (start, count) in enumerate(REGIONS):
            halves = []
            for j in range(2):
                span = pl.ds(EDGE * j + start, count)
                halves.append(shifted(*(strip[i, span, s] for s in slots_of(nbr, i, j, slot, 18 * i + 3 * q))))
            for c in range(3):
                both = jnp.concatenate([halves[0][c], halves[1][c]], axis=1)
                row_view[c, start : start + count] = both.astype(jnp.bfloat16)
        x = (0, nx - 1)[i]
        masks = jnp.stack(mask_of(occ, x, slot, range(ny)))
        own_t = pair_row(lz, feat, masks, i, x, slot).T.astype(jnp.bfloat16)
        for b in range(3):
            pieces = [row_view[c, 2 - b : 2 - b + EDGE].reshape(EDGE * ROWS, WIDTH) for c in range(3)]
            product(own_t, pieces, 18 - 18 * i + 3 * b)
        for j in range(2):
            for p, (start, count) in enumerate(REGIONS):
                span = pl.ds(EDGE * i + start, count)
                moved = shifted(*(side[j, span, s] for s in slots_of(nbr, i, j, slot, 9 * p + 6 * j)))
                for c in range(3):
                    side_view[c, start : start + count] = moved[c]
            y = (0, ny - 1)[j]
            masks = jnp.stack([mask_of(occ, EDGE * i + xl, slot, (y,))[0] for xl in range(EDGE)])
            rows = feat[EDGE * i : EDGE * i + EDGE, y, slot]
            own_t = kept(rows, masks, live_at(lz, i, j, slot)).reshape(EDGE * EDGE, WIDTH)
            own_t = own_t.T.astype(jnp.bfloat16)
            for a in range(3):
                pieces = [side_view[c, 2 - a : 2 - a + EDGE].reshape(EDGE * EDGE, WIDTH) for c in range(3)]
                product(own_t, pieces, 9 * a + 6 - 6 * j)

    for i in range(2):

        def slots(slot, carry, i=i):
            @pl.when(pair_live(lz, i, slot))
            def _():
                unit(i, slot)

            return carry

        lax.fori_loop(0, 2, slots, 0)
    here = core[0]
    chunk = theirs.shape[1] - EDGE
    mine[...] = total[here]
    for n in range(theirs.shape[0]):
        encode(total[1 - here, n * chunk : n * chunk + chunk], theirs, (n,))


def feature_kernel(i, nbr, lz, grad, occ, halo, kernel, *refs):
    out, field, masks, view, acc = refs[-5:]
    ny = grad.shape[1]
    fill_field(i, grad, occ, halo, field, masks)

    def unit(slot, carry):
        live = pair_live(lz, i, slot)

        @pl.when(live)
        def _():
            fill_view(nbr, field, view, i, slot)
            weights = jnp.concatenate([kernel[k] for k in range(27)], axis=1)
            acc[...] = lax.dot_general(
                columns_of(view), weights, (((1,), (1,)), ((), ())), preferred_element_type=jnp.float32
            )

            def emit(xl, c2):
                block = acc[pl.ds(pl.multiple_of(xl * EDGE * ROWS, EDGE * ROWS), EDGE * ROWS), :]
                block = block.reshape(EDGE, 2, EDGE, WIDTH)
                for j in range(2):
                    span = slice(EDGE * j, EDGE * j + EDGE)
                    value = kept(block[:, j], masks[xl + 1, span, slot], live_at(lz, i, j, slot))
                    out[xl, span, slot] = value.astype(jnp.bfloat16)
                return c2

            lax.fori_loop(0, EDGE, emit, 0)

        @pl.when(jnp.logical_not(live))
        def _():
            def blank(xl, c2):
                out[xl, :, slot] = jnp.zeros((ny, EDGE, WIDTH), jnp.bfloat16)
                return c2

            lax.fori_loop(0, EDGE, blank, 0)

        return carry

    lax.fori_loop(0, 2, unit, 0)


def encode(value, coded, places):
    rows = value.shape[0]
    peak = jnp.max(jnp.abs(value), axis=0, keepdims=True)
    power = jnp.floor(jnp.log2(jnp.maximum(peak, 1e-30)) + 1.001)
    code = jnp.clip(jnp.round(value * jnp.exp2(15.0 - power)), -32767.0, 32767.0)
    code = code.astype(jnp.int32).astype(jnp.int16)
    power = jnp.broadcast_to(power, (EDGE, WIDTH)).astype(jnp.int32).astype(jnp.int16)
    for place in places:
        coded[place, 0:rows] = code
        coded[place, rows : rows + EDGE] = power


def decode(coded):
    rows = coded.shape[0] - EDGE
    power = coded[rows:].astype(jnp.int32).astype(jnp.float32)[0:1]
    return coded[:rows].astype(jnp.int32).astype(jnp.float32) * jnp.exp2(power - 15.0)


def encode_half_kernel(mine, theirs, coded):
    chunk = coded.shape[1] - EDGE
    for n in range(coded.shape[0]):
        encode(mine[n * chunk : n * chunk + chunk] + decode(theirs[n]), coded, (n,))


def sum_kernel(scale, coded, again):
    total = decode(coded[0])
    for n in range(1, coded.shape[0]):
        total = total + decode(coded[n])
    encode(total * scale, again, range(again.shape[0]))


def decode_kernel(core, mine, theirs, out):
    chunk = mine.shape[1] - EDGE
    here = core[0]
    for base, coded in ((here * HALF, mine), ((1 - here) * HALF, theirs)):
        for n in range(coded.shape[0]):
            rows = min(chunk, HALF - n * chunk)
            out[pl.ds(pl.multiple_of(base + n * chunk, EDGE), rows)] = decode(coded[n])[0:rows]


SMEM = pl.BlockSpec(memory_space=pltpu.SMEM)
VMEM = pl.BlockSpec(memory_space=pltpu.VMEM)


def call(kernel, name, out_shape, scratch=(), scalars=0, flops=0, nbytes=4 << 20):
    def run(*args):
        return pl.pallas_call(
            kernel,
            out_shape=out_shape,
            in_specs=[SMEM] * scalars + [VMEM] * (len(args) - scalars),
            out_specs=jax.tree.map(lambda _: VMEM, out_shape),
            scratch_shapes=list(scratch),
            compiler_params=pltpu.CompilerParams(vmem_limit_bytes=20 << 20),
            cost_estimate=pl.CostEstimate(flops=flops, bytes_accessed=nbytes, transcendentals=0),
            name=name,
        )(*args)

    return run


def features_call(i, args, scratch, flops, before=None):
    grad = args[2]
    block = (EDGE,) + grad.shape[1:]
    specs = [SMEM, SMEM] + [VMEM] * (len(args) - 2)
    if before is not None:
        args = args + (before,)
        specs.append(pl.BlockSpec(memory_space=pl.ANY))
    return pl.pallas_call(
        lambda *refs: feature_kernel(i, *refs),
        grid=(1,),
        out_shape=jax.ShapeDtypeStruct(grad.shape, jnp.bfloat16),
        in_specs=specs,
        out_specs=pl.BlockSpec(block, lambda g: (i, 0, 0, 0, 0)),
        scratch_shapes=list(scratch),
        input_output_aliases={} if before is None else {len(args) - 1: 0},
        compiler_params=pltpu.CompilerParams(vmem_limit_bytes=20 << 20),
        cost_estimate=pl.CostEstimate(flops=flops, bytes_accessed=4 << 20, transcendentals=0),
        name="conv_features",
    )(*args)


def pack_edges(occ, grad):
    nx, ny = grad.shape[0], grad.shape[1]
    row = (1,) + grad.shape[1:]
    side = (nx, 1) + grad.shape[2:]
    places = ((row, (0, 0)), (row, (nx - 1, 0)), (side, (0, 0)), (side, (0, ny - 1)))
    specs = [pl.BlockSpec(shape, lambda g, at=at: at + (0, 0, 0)) for shape, at in places]
    shapes = [jax.ShapeDtypeStruct(shape, jnp.bfloat16) for shape in (row, row, side, side)]
    whole = [pl.BlockSpec(shape.shape, lambda g: (0, 0, 0, 0, 0)) for shape in shapes]
    return pl.pallas_call(
        pack_kernel,
        grid=(1,),
        out_shape=shapes,
        in_specs=[pl.BlockSpec(occ.shape, lambda g: (0, 0, 0, 0))] + specs,
        out_specs=whole,
        cost_estimate=pl.CostEstimate(flops=0, bytes_accessed=1 << 20, transcendentals=0),
        name="pack_edges",
    )(occ, grad, grad, grad, grad)


def exchange(blocks, axis):
    return lax.all_to_all(blocks, axis, 0, 0)


def local(features, grad_out, occupancy, leaf_z, neighbours, kernel):
    nx, ny = grad_out.shape[1], grad_out.shape[2]
    grad = grad_out[0]
    feat = features[0]
    occ = jnp.transpose(occupancy[0], (0, 2, 3, 1))
    gx, gy = lax.axis_size("gx"), lax.axis_size("gy")
    core = lax.axis_index("dcn").astype(jnp.int32).reshape(1)
    scale = 1.0 / math.sqrt(lax.axis_size("dcn") * gx * gy * nx * ny * 2 * EDGE)
    field = pltpu.VMEM((VIEW, ny + 2, 3, EDGE, WIDTH), jnp.float32)
    masks = pltpu.VMEM((VIEW, ny, 2, EDGE, WIDTH), jnp.float32)
    view = pltpu.VMEM((3, VIEW, VIEW, ROWS, WIDTH), jnp.bfloat16)
    own = pltpu.VMEM((EDGE, EDGE * ROWS, WIDTH), jnp.bfloat16)
    acc = pltpu.VMEM((UNIT, WIDTH), jnp.float32)
    product = 2 * 2 * 512 * 27 * WIDTH * WIDTH

    def shift(block, axis, step):
        count = lax.axis_size(axis)
        pairs = [(i, i + step) for i in range(count) if 0 <= i + step < count]
        return lax.ppermute(block, axis, pairs)

    def coded(count):
        return jax.ShapeDtypeStruct((count, PADDED // gy + EDGE, WIDTH), jnp.int16)

    def terms_of(i, *before):
        return call(
            lambda *refs: terms_kernel(i, *refs),
            "conv_terms",
            jax.ShapeDtypeStruct((2, PADDED, WIDTH), jnp.float32),
            (field, masks, view, own),
            scalars=2,
            flops=product,
        )(neighbours, leaf_z, grad, feat, occ, *before)

    core, packed = lax.optimization_barrier((core, pack_edges(occ, grad)))
    last, first, end, start = packed
    top = shift(last, "gx", 1)
    bottom = shift(first, "gx", -1)
    terms = terms_of(0)
    top, bottom, terms = lax.optimization_barrier((top, bottom, terms))
    side = jax.ShapeDtypeStruct((nx + 2, 1, 2, EDGE, WIDTH), jnp.bfloat16)
    end, start = call(sides_kernel, "pack_sides", (side, side), nbytes=1 << 17)(top, bottom, end, start)
    left = shift(end, "gy", 1)
    right = shift(start, "gy", -1)
    terms = terms_of(1, terms)
    edges = (top, bottom, left, right)
    mine, theirs, halo = call(
        edge_kernel,
        "edge_terms",
        (
            jax.ShapeDtypeStruct((PADDED, WIDTH), jnp.float32),
            coded(gy),
            jax.ShapeDtypeStruct((2 * (nx + ny + 2), 2, EDGE, WIDTH), jnp.bfloat16),
        ),
        (
            pltpu.VMEM((2, PADDED, WIDTH), jnp.float32),
            pltpu.VMEM((2, ny + 2, 3, EDGE, WIDTH), jnp.float32),
            pltpu.VMEM((2, nx + 2, 3, EDGE, WIDTH), jnp.float32),
            pltpu.VMEM((3, VIEW, ROWS, WIDTH), jnp.bfloat16),
            pltpu.VMEM((3, VIEW, EDGE, WIDTH), jnp.float32),
        ),
        scalars=3,
        flops=product // 4,
    )(neighbours, leaf_z, core, feat, occ, *edges, terms)
    theirs = lax.ppermute(theirs, "dcn", [(0, 1), (1, 0)])
    half = call(encode_half_kernel, "encode_half", coded(gy), nbytes=2 << 20)(mine, theirs)

    def features_part(i, value, *before):
        late, value = lax.optimization_barrier((grad, value))
        args = (neighbours, leaf_z, late, occ, halo, kernel)
        return features_call(i, args, (field, masks, view, acc), product, *before), value

    half = exchange(half, "gy")
    piece = call(lambda c, o: sum_kernel(1.0, c, o), "sum_piece", coded(gx), nbytes=1 << 20)(half)
    out, piece = features_part(0, piece)
    piece, out = lax.optimization_barrier((exchange(piece, "gx"), out))
    total = call(lambda c, o: sum_kernel(scale, c, o), "sum_total", coded(gy), nbytes=1 << 20)(piece)
    out, total = features_part(1, total, out)
    total, out = lax.optimization_barrier((exchange(total, "gy"), out))
    other = lax.ppermute(total, "dcn", [(0, 1), (1, 0)])
    kernel_grad = call(
        decode_kernel,
        "decode_total",
        jax.ShapeDtypeStruct((27 * WIDTH, WIDTH), jnp.float32),
        scalars=1,
        nbytes=3 << 20,
    )(core, total, other)
    return out[None], kernel_grad.reshape(27, WIDTH, WIDTH)


def solution(mesh):
    return jax.shard_map(
        local,
        mesh=mesh,
        in_specs=(
            P("dcn", "gx", "gy", None, None, None),
            P("dcn", "gx", "gy", None, None, None),
            P("dcn", "gx", "gy", None, None),
            P("dcn", "gx", "gy", None),
            P("dcn", "gx", "gy", None, None),
            P(),
        ),
        out_specs=(P("dcn", "gx", "gy", None, None, None), P()),
        check_vma=False,
    )
```

```python
import math

import jax
import jax.numpy as jnp
from jax import lax
from jax.experimental import pallas as pl
from jax.experimental.pallas import tpu as pltpu
from jax.sharding import PartitionSpec as P

EDGE = 8
WIDTH = 128
VIEW = EDGE + 2
ROWS = 2 * EDGE
UNIT = EDGE * EDGE * ROWS
HALF = 27 * WIDTH // 2
PADDED = 1792


def shifted(below, here, above):
    row = lax.broadcasted_iota(jnp.int32, here.shape, 1)
    return (
        pltpu.roll(jnp.where(row == 0, above, here), EDGE - 1, 1),
        here,
        pltpu.roll(jnp.where(row == EDGE - 1, below, here), 1, 1),
    )


REGIONS = ((0, 1), (1, EDGE), (EDGE + 1, 1))


def slots_of(nbr, i, j, slot, first):
    return [nbr[0, i, j, slot, first + r] for r in range(3)]


def live_at(lz, i, j, slot):
    return lz[0, i, j, slot] >= 0


def pair_live(lz, i, slot):
    return jnp.logical_or(live_at(lz, i, 0, slot), live_at(lz, i, 1, slot))


def kept(value, mask, live):
    return value.astype(jnp.float32) * (mask * live.astype(jnp.float32))


def mask_of(occ, x, slot, spots):
    tile = occ[x, slot].astype(jnp.float32)
    return [jnp.broadcast_to(tile[:, y : y + 1], (EDGE, WIDTH)) for y in spots]


def pack_kernel(low, high, first, last, top, bottom):
    for occ, source, target in ((low, first, bottom), (high, last, top)):
        for slot in range(2):
            for y, mask in enumerate(mask_of(occ, 0, slot, range(occ.shape[3]))):
                target[0, y, slot] = (source[0, y, slot].astype(jnp.float32) * mask).astype(jnp.bfloat16)


def own_sides_kernel(occ, grad, left, right):
    nx, ny = occ.shape[0], occ.shape[3]
    for x in range(nx):
        for slot in range(2):
            for target, y in ((left, ny - 1), (right, 0)):
                mask = mask_of(occ, x, slot, (y,))[0]
                target[x, 0, slot] = (grad[x, y, slot].astype(jnp.float32) * mask).astype(jnp.bfloat16)


def sides_kernel(top, bottom, left, right, left_side, right_side):
    nx, ny = left.shape[0], top.shape[1]
    for own, side, y in ((left, left_side, ny - 1), (right, right_side, 0)):
        side[0, 0] = top[0, y]
        side[1 : nx + 1] = own[...]
        side[nx + 1, 0] = bottom[0, y]


def fill_field(i, grad, occ, halo, field, masks):
    nx, ny = grad.shape[0], grad.shape[1]
    low, high = (1, VIEW) if i == 0 else (0, VIEW - 1)

    for r in range(low, high):
        x = EDGE * i - 1 + r
        values = grad[x].astype(jnp.float32)
        for slot in range(2):
            for y, mask in enumerate(mask_of(occ, x, slot, range(ny))):
                masks[r, y, slot] = mask
                field[r, y + 1, slot] = values[y, slot] * mask
    outer = 0 if i == 0 else VIEW - 1
    field[:, :, 2] = jnp.zeros((VIEW, ny + 2, EDGE, WIDTH), jnp.float32)
    if halo is None:
        field[outer, :, 0:2] = jnp.zeros((ny + 2, 2, EDGE, WIDTH), jnp.float32)
        field[:, 0, 0:2] = jnp.zeros((VIEW, 2, EDGE, WIDTH), jnp.float32)
        field[:, ny + 1, 0:2] = jnp.zeros((VIEW, 2, EDGE, WIDTH), jnp.float32)
    else:
        left = 2 * ny + EDGE * i
        right = left + nx + 2
        field[outer, 1 : ny + 1, 0:2] = halo[ny * i : ny * i + ny].astype(jnp.float32)
        field[:, 0, 0:2] = halo[left : left + VIEW].astype(jnp.float32)
        field[:, ny + 1, 0:2] = halo[right : right + VIEW].astype(jnp.float32)


def fill_view(nbr, field, view, i, slot):
    def view_rows(xl, p):
        for q, (start, count) in enumerate(REGIONS):
            halves = []
            for j in range(2):
                span = pl.ds(EDGE * j + start, count)
                halves.append(shifted(*(field[xl, span, s] for s in slots_of(nbr, i, j, slot, 9 * p + 3 * q))))
            for c in range(3):
                both = jnp.concatenate([halves[0][c], halves[1][c]], axis=1)
                view[c, xl, start : start + count] = both.astype(jnp.bfloat16)

    for p, (start, count) in enumerate(REGIONS):
        for xl in range(start, start + count):
            view_rows(xl, p)


def columns_of(view):
    pieces = [
        view[c, 2 - a : 2 - a + EDGE, 2 - b : 2 - b + EDGE].reshape(UNIT, WIDTH)
        for a in range(3)
        for b in range(3)
        for c in range(3)
    ]
    return jnp.concatenate(pieces, axis=1)


def pair_row(lz, feat, masks, i, x, slot):
    pair = []
    for j in range(2):
        span = slice(EDGE * j, EDGE * j + EDGE)
        pair.append(kept(feat[x, span, slot], masks[span], live_at(lz, i, j, slot)))
    return jnp.concatenate(pair, axis=1).reshape(EDGE * ROWS, WIDTH)


def add_terms(total, first, part):
    for c in range(3):
        for s in range(2):
            half = 2 * (first + c) + s
            core, start = half // 27, half * 64 - half // 27 * HALF
            total[core, start : start + 64] += part[s * 64 : s * 64 + 64, c * WIDTH : (c + 1) * WIDTH]


def terms_kernel(i, nbr, lz, grad, feat, occ, *refs):
    *before, terms, field, masks, view, own = refs
    terms[...] = before[0][...] if before else jnp.zeros_like(terms)
    fill_field(i, grad, occ, None, field, masks)

    def unit(slot, carry):
        @pl.when(pair_live(lz, i, slot))
        def _():
            fill_view(nbr, field, view, i, slot)

            for xl in range(EDGE):
                rows = pair_row(lz, feat, masks[xl + 1, :, slot], i, EDGE * i + xl, slot)
                own[xl] = rows.astype(jnp.bfloat16)
            own_t = own[...].reshape(UNIT, WIDTH).T
            part = jnp.dot(own_t, columns_of(view), preferred_element_type=jnp.float32)
            for k in range(0, 27, 3):
                add_terms(terms, k, part[:, k * WIDTH : (k + 3) * WIDTH])

        return carry

    lax.fori_loop(0, 2, unit, 0)


def edge_kernel(nbr, lz, core, feat, occ, top, bottom, left, right, before, mine, theirs, halo, total, strip, side, row_view, side_view):
    nx, ny = feat.shape[0], feat.shape[1]
    total[...] = before[...]
    halo[0:ny] = top[0]
    halo[ny : 2 * ny] = bottom[0]
    halo[2 * ny : 2 * ny + nx + 2] = left[:, 0]
    halo[2 * ny + nx + 2 :] = right[:, 0]
    for i in range(2):
        spot = (0, nx + 1)[i]
        strip[i, 1 : ny + 1, 0:2] = (top, bottom)[i][0].astype(jnp.float32)
        strip[i, 0, 0:2] = left[spot, 0].astype(jnp.float32)
        strip[i, ny + 1, 0:2] = right[spot, 0].astype(jnp.float32)
        side[i, 1 : nx + 1, 0:2] = (left, right)[i][1 : nx + 1, 0].astype(jnp.float32)
        for end in (0, nx + 1):
            side[i, end, 0:2] = jnp.zeros((2, EDGE, WIDTH), jnp.float32)
    strip[:, :, 2] = jnp.zeros((2, ny + 2, EDGE, WIDTH), jnp.float32)
    side[:, :, 2] = jnp.zeros((2, nx + 2, EDGE, WIDTH), jnp.float32)

    def product(own_t, pieces, firsts):
        columns = jnp.concatenate(pieces, axis=1).astype(jnp.bfloat16)
        part = jnp.dot(own_t, columns, preferred_element_type=jnp.float32)
        for n, first in enumerate(firsts):
            add_terms(total, first, part[:, 3 * n * WIDTH : 3 * (n + 1) * WIDTH])

    def unit(i, slot):
        for q, (start, count) in enumerate(REGIONS):
            halves = []
            for j in range(2):
                span = pl.ds(EDGE * j + start, count)
                halves.append(shifted(*(strip[i, span, s] for s in slots_of(nbr, i, j, slot, 18 * i + 3 * q))))
            for c in range(3):
                both = jnp.concatenate([halves[0][c], halves[1][c]], axis=1)
                row_view[c, start : start + count] = both.astype(jnp.bfloat16)
        x = (0, nx - 1)[i]
        masks = jnp.stack(mask_of(occ, x, slot, range(ny)))
        own_t = pair_row(lz, feat, masks, i, x, slot).T.astype(jnp.bfloat16)
        pieces = [
            row_view[c, 2 - b : 2 - b + EDGE].reshape(EDGE * ROWS, WIDTH) for b in range(3) for c in range(3)
        ]
        product(own_t, pieces, [18 - 18 * i + 3 * b for b in range(3)])
        for j in range(2):
            for p, (start, count) in enumerate(REGIONS):
                span = pl.ds(EDGE * i + start, count)
                moved = shifted(*(side[j, span, s] for s in slots_of(nbr, i, j, slot, 9 * p + 6 * j)))
                for c in range(3):
                    side_view[c, start : start + count] = moved[c]
            y = (0, ny - 1)[j]
            masks = jnp.stack([mask_of(occ, EDGE * i + xl, slot, (y,))[0] for xl in range(EDGE)])
            rows = feat[EDGE * i : EDGE * i + EDGE, y, slot]
            own_t = kept(rows, masks, live_at(lz, i, j, slot)).reshape(EDGE * EDGE, WIDTH)
            own_t = own_t.T.astype(jnp.bfloat16)
            pieces = [
                side_view[c, 2 - a : 2 - a + EDGE].reshape(EDGE * EDGE, WIDTH) for a in range(3) for c in range(3)
            ]
            product(own_t, pieces, [9 * a + 6 - 6 * j for a in range(3)])

    for i in range(2):

        def slots(slot, carry, i=i):
            @pl.when(pair_live(lz, i, slot))
            def _():
                unit(i, slot)

            return carry

        lax.fori_loop(0, 2, slots, 0)
    here = core[0]
    chunk = theirs.shape[1] - EDGE
    mine[...] = total[here]
    for n in range(theirs.shape[0]):
        encode(total[1 - here, n * chunk : n * chunk + chunk], theirs, (n,))


def feature_kernel(i, nbr, lz, grad, occ, halo, kernel, *refs):
    out, field, masks, view, acc = refs[-5:]
    ny = grad.shape[1]
    fill_field(i, grad, occ, halo, field, masks)

    def unit(slot, carry):
        live = pair_live(lz, i, slot)

        @pl.when(live)
        def _():
            fill_view(nbr, field, view, i, slot)
            weights = jnp.concatenate([kernel[k] for k in range(27)], axis=1)
            acc[...] = lax.dot_general(
                columns_of(view), weights, (((1,), (1,)), ((), ())), preferred_element_type=jnp.float32
            )

            for xl in range(EDGE):
                block = acc[xl * EDGE * ROWS : (xl + 1) * EDGE * ROWS].reshape(EDGE, 2, EDGE, WIDTH)
                for j in range(2):
                    span = slice(EDGE * j, EDGE * j + EDGE)
                    value = kept(block[:, j], masks[xl + 1, span, slot], live_at(lz, i, j, slot))
                    out[xl, span, slot] = value.astype(jnp.bfloat16)

        @pl.when(jnp.logical_not(live))
        def _():
            def blank(xl, c2):
                out[xl, :, slot] = jnp.zeros((ny, EDGE, WIDTH), jnp.bfloat16)
                return c2

            lax.fori_loop(0, EDGE, blank, 0)

        return carry

    lax.fori_loop(0, 2, unit, 0)


def encode(value, coded, places):
    rows = value.shape[0]
    peak = jnp.max(jnp.abs(value), axis=0, keepdims=True)
    power = jnp.floor(jnp.log2(jnp.maximum(peak, 1e-30)) + 1.001)
    code = jnp.clip(jnp.round(value * jnp.exp2(15.0 - power)), -32767.0, 32767.0)
    code = code.astype(jnp.int32).astype(jnp.int16)
    power = jnp.broadcast_to(power, (EDGE, WIDTH)).astype(jnp.int32).astype(jnp.int16)
    for place in places:
        coded[place, 0:rows] = code
        coded[place, rows : rows + EDGE] = power


def decode(coded):
    rows = coded.shape[0] - EDGE
    power = coded[rows:].astype(jnp.int32).astype(jnp.float32)[0:1]
    return coded[:rows].astype(jnp.int32).astype(jnp.float32) * jnp.exp2(power - 15.0)


def encode_half_kernel(mine, theirs, coded):
    chunk = coded.shape[1] - EDGE
    for n in range(coded.shape[0]):
        encode(mine[n * chunk : n * chunk + chunk] + decode(theirs[n]), coded, (n,))


def sum_kernel(scale, coded, again):
    total = decode(coded[0])
    for n in range(1, coded.shape[0]):
        total = total + decode(coded[n])
    encode(total * scale, again, range(again.shape[0]))


def decode_kernel(flip, core, coded, *refs):
    out, part, done = refs[-3:]
    chunk = coded.shape[1] - EDGE
    here = core[0] + flip * (1 - 2 * core[0])
    copies = []
    for n in range(coded.shape[0]):
        rows = min(chunk, HALF - n * chunk)
        spot = pl.ds(n * chunk, rows)
        part[spot] = decode(coded[n])[0:rows]
        target = out.at[pl.ds(pl.multiple_of(here * HALF + n * chunk, EDGE), rows)]
        copies.append(pltpu.make_async_copy(part.at[spot], target, done.at[n]))
        copies[-1].start()
    for copy in copies:
        copy.wait()


SMEM = pl.BlockSpec(memory_space=pltpu.SMEM)
VMEM = pl.BlockSpec(memory_space=pltpu.VMEM)


def call(kernel, name, out_shape, scratch=(), scalars=0, flops=0, nbytes=4 << 20):
    def run(*args):
        return pl.pallas_call(
            kernel,
            out_shape=out_shape,
            in_specs=[SMEM] * scalars + [VMEM] * (len(args) - scalars),
            out_specs=jax.tree.map(lambda _: VMEM, out_shape),
            scratch_shapes=list(scratch),
            compiler_params=pltpu.CompilerParams(vmem_limit_bytes=20 << 20),
            cost_estimate=pl.CostEstimate(flops=flops, bytes_accessed=nbytes, transcendentals=0),
            name=name,
        )(*args)

    return run


def features_call(i, args, scratch, flops, before=None):
    grad = args[2]
    block = (EDGE,) + grad.shape[1:]
    specs = [SMEM, SMEM] + [VMEM] * (len(args) - 2)
    if before is not None:
        args = args + (before,)
        specs.append(pl.BlockSpec(memory_space=pl.ANY))
    return pl.pallas_call(
        lambda *refs: feature_kernel(i, *refs),
        grid=(1,),
        out_shape=jax.ShapeDtypeStruct(grad.shape, jnp.bfloat16),
        in_specs=specs,
        out_specs=pl.BlockSpec(block, lambda g: (i, 0, 0, 0, 0)),
        scratch_shapes=list(scratch),
        input_output_aliases={} if before is None else {len(args) - 1: 0},
        compiler_params=pltpu.CompilerParams(vmem_limit_bytes=20 << 20),
        cost_estimate=pl.CostEstimate(flops=flops, bytes_accessed=4 << 20, transcendentals=0),
        name="conv_features",
    )(*args)


def pack_edges(occ, grad):
    row = (1,) + grad.shape[1:]
    tile = (1,) + occ.shape[1:]
    ends = (0, grad.shape[0] - 1)
    tiles = [pl.BlockSpec(tile, lambda g, at=at: (at, 0, 0, 0)) for at in ends]
    rows = [pl.BlockSpec(row, lambda g, at=at: (at, 0, 0, 0, 0)) for at in ends]
    return pl.pallas_call(
        pack_kernel,
        grid=(1,),
        out_shape=[jax.ShapeDtypeStruct(row, jnp.bfloat16)] * 2,
        in_specs=tiles + rows,
        out_specs=[pl.BlockSpec(row, lambda g: (0, 0, 0, 0, 0))] * 2,
        cost_estimate=pl.CostEstimate(flops=0, bytes_accessed=1 << 18, transcendentals=0),
        name="pack_edges",
    )(occ, occ, grad, grad)


def decode_part(core, coded, *before):
    anywhere = pl.BlockSpec(memory_space=pl.ANY)
    flip = len(before)
    return pl.pallas_call(
        lambda *refs: decode_kernel(flip, *refs),
        in_specs=[SMEM, VMEM] + [anywhere] * flip,
        out_specs=anywhere,
        out_shape=jax.ShapeDtypeStruct((2 * HALF, WIDTH), jnp.float32),
        scratch_shapes=[pltpu.VMEM((HALF, WIDTH), jnp.float32), pltpu.SemaphoreType.DMA((coded.shape[0],))],
        input_output_aliases={2: 0} if before else {},
        compiler_params=pltpu.CompilerParams(vmem_limit_bytes=20 << 20),
        cost_estimate=pl.CostEstimate(flops=0, bytes_accessed=3 << 19, transcendentals=0),
        name="decode_half",
    )(core, coded, *before)


def exchange(blocks, axis):
    return lax.all_to_all(blocks, axis, 0, 0)


def local(features, grad_out, occupancy, leaf_z, neighbours, kernel):
    nx, ny = grad_out.shape[1], grad_out.shape[2]
    grad = grad_out[0]
    feat = features[0]
    occ = jnp.transpose(occupancy[0], (0, 2, 3, 1))
    gx, gy = lax.axis_size("gx"), lax.axis_size("gy")
    core = lax.axis_index("dcn").astype(jnp.int32).reshape(1)
    scale = 1.0 / math.sqrt(lax.axis_size("dcn") * gx * gy * nx * ny * 2 * EDGE)
    field = pltpu.VMEM((VIEW, ny + 2, 3, EDGE, WIDTH), jnp.float32)
    masks = pltpu.VMEM((VIEW, ny, 2, EDGE, WIDTH), jnp.float32)
    view = pltpu.VMEM((3, VIEW, VIEW, ROWS, WIDTH), jnp.bfloat16)
    own = pltpu.VMEM((EDGE, EDGE * ROWS, WIDTH), jnp.bfloat16)
    acc = pltpu.VMEM((UNIT, WIDTH), jnp.float32)
    product = 2 * 2 * 512 * 27 * WIDTH * WIDTH

    def shift(block, axis, step):
        count = lax.axis_size(axis)
        pairs = [(i, i + step) for i in range(count) if 0 <= i + step < count]
        return lax.ppermute(block, axis, pairs)

    def coded(count):
        return jax.ShapeDtypeStruct((count, PADDED // gy + EDGE, WIDTH), jnp.int16)

    def terms_of(i, *before):
        return call(
            lambda *refs: terms_kernel(i, *refs),
            "conv_terms",
            jax.ShapeDtypeStruct((2, PADDED, WIDTH), jnp.float32),
            (field, masks, view, own),
            scalars=2,
            flops=product,
        )(neighbours, leaf_z, grad, feat, occ, *before)

    core, packed = lax.optimization_barrier((core, pack_edges(occ, grad)))
    last, first = packed
    top = shift(last, "gx", 1)
    bottom = shift(first, "gx", -1)
    own_side = jax.ShapeDtypeStruct((nx, 1, 2, EDGE, WIDTH), jnp.bfloat16)
    end, start = call(own_sides_kernel, "own_sides", (own_side, own_side), nbytes=1 << 19)(occ, grad)
    terms = terms_of(0)
    top, bottom, terms = lax.optimization_barrier((top, bottom, terms))
    side = jax.ShapeDtypeStruct((nx + 2, 1, 2, EDGE, WIDTH), jnp.bfloat16)
    end, start = call(sides_kernel, "pack_sides", (side, side), nbytes=1 << 17)(top, bottom, end, start)
    left = shift(end, "gy", 1)
    right = shift(start, "gy", -1)
    terms = terms_of(1, terms)
    edges = (top, bottom, left, right)
    mine, theirs, halo = call(
        edge_kernel,
        "edge_terms",
        (
            jax.ShapeDtypeStruct((PADDED, WIDTH), jnp.float32),
            coded(gy),
            jax.ShapeDtypeStruct((2 * (nx + ny + 2), 2, EDGE, WIDTH), jnp.bfloat16),
        ),
        (
            pltpu.VMEM((2, PADDED, WIDTH), jnp.float32),
            pltpu.VMEM((2, ny + 2, 3, EDGE, WIDTH), jnp.float32),
            pltpu.VMEM((2, nx + 2, 3, EDGE, WIDTH), jnp.float32),
            pltpu.VMEM((3, VIEW, ROWS, WIDTH), jnp.bfloat16),
            pltpu.VMEM((3, VIEW, EDGE, WIDTH), jnp.float32),
        ),
        scalars=3,
        flops=product // 4,
    )(neighbours, leaf_z, core, feat, occ, *edges, terms)
    theirs = lax.ppermute(theirs, "dcn", [(0, 1), (1, 0)])
    half = call(encode_half_kernel, "encode_half", coded(gy), nbytes=2 << 20)(mine, theirs)

    def features_part(i, value, *before):
        late, value = lax.optimization_barrier((grad, value))
        args = (neighbours, leaf_z, late, occ, halo, kernel)
        return features_call(i, args, (field, masks, view, acc), product, *before), value

    half = exchange(half, "gy")
    piece = call(lambda c, o: sum_kernel(1.0, c, o), "sum_piece", coded(gx), nbytes=1 << 20)(half)
    out, piece = features_part(0, piece)
    piece, out = lax.optimization_barrier((exchange(piece, "gx"), out))
    total = call(lambda c, o: sum_kernel(scale, c, o), "sum_total", coded(gy), nbytes=1 << 20)(piece)
    out, total = features_part(1, total, out)
    total, out = lax.optimization_barrier((exchange(total, "gy"), out))
    other = lax.ppermute(total, "dcn", [(0, 1), (1, 0)])
    kernel_grad = decode_part(core, other, decode_part(core, total))
    return out[None], kernel_grad.reshape(27, WIDTH, WIDTH)


def solution(mesh):
    return jax.shard_map(
        local,
        mesh=mesh,
        in_specs=(
            P("dcn", "gx", "gy", None, None, None),
            P("dcn", "gx", "gy", None, None, None),
            P("dcn", "gx", "gy", None, None),
            P("dcn", "gx", "gy", None),
            P("dcn", "gx", "gy", None, None),
            P(),
        ),
        out_specs=(P("dcn", "gx", "gy", None, None, None), P()),
        check_vma=False,
    )
```

```python
import math

import jax
import jax.numpy as jnp
from jax import lax
from jax.experimental import pallas as pl
from jax.experimental.pallas import tpu as pltpu
from jax.sharding import PartitionSpec as P

EDGE = 8
WIDTH = 128
VIEW = EDGE + 2
ROWS = 2 * EDGE
UNIT = EDGE * EDGE * ROWS
HALF = 27 * WIDTH // 2
PADDED = 1792


def shifted(below, here, above):
    row = lax.broadcasted_iota(jnp.int32, here.shape, 1)
    return (
        pltpu.roll(jnp.where(row == 0, above, here), EDGE - 1, 1),
        here,
        pltpu.roll(jnp.where(row == EDGE - 1, below, here), 1, 1),
    )


REGIONS = ((0, 1), (1, EDGE), (EDGE + 1, 1))


def slots_of(nbr, i, j, slot, first):
    return [nbr[0, i, j, slot, first + r] for r in range(3)]


def live_at(lz, i, j, slot):
    return lz[0, i, j, slot] >= 0


def pair_live(lz, i, slot):
    return jnp.logical_or(live_at(lz, i, 0, slot), live_at(lz, i, 1, slot))


def kept(value, mask, live):
    return value.astype(jnp.float32) * (mask * live.astype(jnp.float32))


def mask_of(occ, x, slot, spots):
    tile = occ[x, slot].astype(jnp.float32)
    return [jnp.broadcast_to(tile[:, y : y + 1], (EDGE, WIDTH)) for y in spots]


def pack_kernel(low, high, first, last, top, bottom):
    for occ, source, target in ((low, first, bottom), (high, last, top)):
        for slot in range(2):
            for y, mask in enumerate(mask_of(occ, 0, slot, range(occ.shape[3]))):
                target[0, y, slot] = (source[0, y, slot].astype(jnp.float32) * mask).astype(jnp.bfloat16)


def own_sides_kernel(occ, grad, left, right):
    nx, ny = occ.shape[0], occ.shape[3]
    for x in range(nx):
        for slot in range(2):
            for target, y in ((left, ny - 1), (right, 0)):
                mask = mask_of(occ, x, slot, (y,))[0]
                target[x, 0, slot] = (grad[x, y, slot].astype(jnp.float32) * mask).astype(jnp.bfloat16)


def sides_kernel(top, bottom, left, right, left_side, right_side):
    nx, ny = left.shape[0], top.shape[1]
    for own, side, y in ((left, left_side, ny - 1), (right, right_side, 0)):
        side[0, 0] = top[0, y]
        side[1 : nx + 1] = own[...]
        side[nx + 1, 0] = bottom[0, y]


def fill_field(i, grad, occ, halo, field, masks):
    nx, ny = grad.shape[0], grad.shape[1]
    low, high = (1, VIEW) if i == 0 else (0, VIEW - 1)

    for r in range(low, high):
        x = EDGE * i - 1 + r
        values = grad[x].astype(jnp.float32)
        for slot in range(2):
            for y, mask in enumerate(mask_of(occ, x, slot, range(ny))):
                masks[r, y, slot] = mask
                field[r, y + 1, slot] = values[y, slot] * mask
    outer = 0 if i == 0 else VIEW - 1
    field[:, :, 2] = jnp.zeros((VIEW, ny + 2, EDGE, WIDTH), jnp.float32)
    if halo is None:
        field[outer, :, 0:2] = jnp.zeros((ny + 2, 2, EDGE, WIDTH), jnp.float32)
        field[:, 0, 0:2] = jnp.zeros((VIEW, 2, EDGE, WIDTH), jnp.float32)
        field[:, ny + 1, 0:2] = jnp.zeros((VIEW, 2, EDGE, WIDTH), jnp.float32)
    else:
        left = 2 * ny + EDGE * i
        right = left + nx + 2
        field[outer, 1 : ny + 1, 0:2] = halo[ny * i : ny * i + ny].astype(jnp.float32)
        field[:, 0, 0:2] = halo[left : left + VIEW].astype(jnp.float32)
        field[:, ny + 1, 0:2] = halo[right : right + VIEW].astype(jnp.float32)


def fill_view(nbr, field, view, i, slot):
    def view_rows(xl, p):
        for q, (start, count) in enumerate(REGIONS):
            halves = []
            for j in range(2):
                span = pl.ds(EDGE * j + start, count)
                halves.append(shifted(*(field[xl, span, s] for s in slots_of(nbr, i, j, slot, 9 * p + 3 * q))))
            for c in range(3):
                both = jnp.concatenate([halves[0][c], halves[1][c]], axis=1)
                view[c, xl, start : start + count] = both.astype(jnp.bfloat16)

    for p, (start, count) in enumerate(REGIONS):
        for xl in range(start, start + count):
            view_rows(xl, p)


def columns_of(view):
    pieces = [
        view[c, 2 - a : 2 - a + EDGE, 2 - b : 2 - b + EDGE].reshape(UNIT, WIDTH)
        for a in range(3)
        for b in range(3)
        for c in range(3)
    ]
    return jnp.concatenate(pieces, axis=1)


def pair_row(lz, feat, masks, i, x, slot):
    pair = []
    for j in range(2):
        span = slice(EDGE * j, EDGE * j + EDGE)
        pair.append(kept(feat[x, span, slot], masks[span], live_at(lz, i, j, slot)))
    return jnp.concatenate(pair, axis=1).reshape(EDGE * ROWS, WIDTH)


def add_terms(total, first, part):
    for c in range(3):
        for s in range(2):
            half = 2 * (first + c) + s
            core, start = half // 27, half * 64 - half // 27 * HALF
            total[core, start : start + 64] += part[s * 64 : s * 64 + 64, c * WIDTH : (c + 1) * WIDTH]


def terms_kernel(i, nbr, lz, grad, feat, occ, *refs):
    *before, terms, field, masks, view, own, strip, row_view = refs
    terms[...] = before[2][...] if before else jnp.zeros_like(terms)
    if before:
        row_edges(nbr, lz, feat, occ, before[0], before[1], terms, strip, row_view)
    fill_field(i, grad, occ, None, field, masks)

    def unit(slot, carry):
        @pl.when(pair_live(lz, i, slot))
        def _():
            fill_view(nbr, field, view, i, slot)

            for xl in range(EDGE):
                rows = pair_row(lz, feat, masks[xl + 1, :, slot], i, EDGE * i + xl, slot)
                own[xl] = rows.astype(jnp.bfloat16)
            own_t = own[...].reshape(UNIT, WIDTH).T
            part = jnp.dot(own_t, columns_of(view), preferred_element_type=jnp.float32)
            for k in range(0, 27, 3):
                add_terms(terms, k, part[:, k * WIDTH : (k + 3) * WIDTH])

        return carry

    lax.fori_loop(0, 2, unit, 0)


def product(total, own_t, pieces, firsts):
    columns = jnp.concatenate(pieces, axis=1).astype(jnp.bfloat16)
    part = jnp.dot(own_t, columns, preferred_element_type=jnp.float32)
    for n, first in enumerate(firsts):
        add_terms(total, first, part[:, 3 * n * WIDTH : 3 * (n + 1) * WIDTH])


def row_edges(nbr, lz, feat, occ, top, bottom, total, strip, row_view):
    nx, ny = feat.shape[0], feat.shape[1]
    for i in range(2):
        strip[i, 1 : ny + 1, 0:2] = (top, bottom)[i][0].astype(jnp.float32)
        for end in (0, ny + 1):
            strip[i, end, 0:2] = jnp.zeros((2, EDGE, WIDTH), jnp.float32)
    strip[:, :, 2] = jnp.zeros((2, ny + 2, EDGE, WIDTH), jnp.float32)

    def unit(i, slot):
        for q, (start, count) in enumerate(REGIONS):
            halves = []
            for j in range(2):
                span = pl.ds(EDGE * j + start, count)
                halves.append(shifted(*(strip[i, span, s] for s in slots_of(nbr, i, j, slot, 18 * i + 3 * q))))
            for c in range(3):
                both = jnp.concatenate([halves[0][c], halves[1][c]], axis=1)
                row_view[c, start : start + count] = both.astype(jnp.bfloat16)
        x = (0, nx - 1)[i]
        masks = jnp.stack(mask_of(occ, x, slot, range(ny)))
        own_t = pair_row(lz, feat, masks, i, x, slot).T.astype(jnp.bfloat16)
        pieces = [
            row_view[c, 2 - b : 2 - b + EDGE].reshape(EDGE * ROWS, WIDTH) for b in range(3) for c in range(3)
        ]
        product(total, own_t, pieces, [18 - 18 * i + 3 * b for b in range(3)])

    for_live(lz, unit)


def for_live(lz, unit):
    for i in range(2):

        def slots(slot, carry, i=i):
            @pl.when(pair_live(lz, i, slot))
            def _():
                unit(i, slot)

            return carry

        lax.fori_loop(0, 2, slots, 0)


def edge_kernel(nbr, lz, core, feat, occ, top, bottom, left, right, before, mine, theirs, halo, total, side, side_view):
    nx, ny = feat.shape[0], feat.shape[1]
    total[...] = before[...]
    halo[0:ny] = top[0]
    halo[ny : 2 * ny] = bottom[0]
    halo[2 * ny : 2 * ny + nx + 2] = left[:, 0]
    halo[2 * ny + nx + 2 :] = right[:, 0]
    for j in range(2):
        side[j, :, 0:2] = (left, right)[j][:, 0].astype(jnp.float32)
    side[:, :, 2] = jnp.zeros((2, nx + 2, EDGE, WIDTH), jnp.float32)

    def unit(i, slot):
        for j in range(2):
            for p, (start, count) in enumerate(REGIONS):
                span = pl.ds(EDGE * i + start, count)
                moved = shifted(*(side[j, span, s] for s in slots_of(nbr, i, j, slot, 9 * p + 6 * j)))
                for c in range(3):
                    side_view[c, start : start + count] = moved[c]
            y = (0, ny - 1)[j]
            masks = jnp.stack([mask_of(occ, EDGE * i + xl, slot, (y,))[0] for xl in range(EDGE)])
            rows = feat[EDGE * i : EDGE * i + EDGE, y, slot]
            own_t = kept(rows, masks, live_at(lz, i, j, slot)).reshape(EDGE * EDGE, WIDTH)
            own_t = own_t.T.astype(jnp.bfloat16)
            pieces = [
                side_view[c, 2 - a : 2 - a + EDGE].reshape(EDGE * EDGE, WIDTH) for a in range(3) for c in range(3)
            ]
            product(total, own_t, pieces, [9 * a + 6 - 6 * j for a in range(3)])

    for_live(lz, unit)
    here = core[0]
    chunk = theirs.shape[1] - EDGE
    mine[...] = total[here]
    for n in range(theirs.shape[0]):
        encode(total[1 - here, n * chunk : n * chunk + chunk], theirs, (n,))


def feature_kernel(i, nbr, lz, grad, occ, halo, kernel, *refs):
    out, field, masks, view, acc = refs[-5:]
    ny = grad.shape[1]
    fill_field(i, grad, occ, halo, field, masks)

    def unit(slot, carry):
        live = pair_live(lz, i, slot)

        @pl.when(live)
        def _():
            fill_view(nbr, field, view, i, slot)
            weights = jnp.concatenate([kernel[k] for k in range(27)], axis=1)
            acc[...] = lax.dot_general(
                columns_of(view), weights, (((1,), (1,)), ((), ())), preferred_element_type=jnp.float32
            )

            for xl in range(EDGE):
                block = acc[xl * EDGE * ROWS : (xl + 1) * EDGE * ROWS].reshape(EDGE, 2, EDGE, WIDTH)
                for j in range(2):
                    span = slice(EDGE * j, EDGE * j + EDGE)
                    value = kept(block[:, j], masks[xl + 1, span, slot], live_at(lz, i, j, slot))
                    out[xl, span, slot] = value.astype(jnp.bfloat16)

        @pl.when(jnp.logical_not(live))
        def _():
            def blank(xl, c2):
                out[xl, :, slot] = jnp.zeros((ny, EDGE, WIDTH), jnp.bfloat16)
                return c2

            lax.fori_loop(0, EDGE, blank, 0)

        return carry

    lax.fori_loop(0, 2, unit, 0)


def encode(value, coded, places):
    rows = value.shape[0]
    peak = jnp.max(jnp.abs(value), axis=0, keepdims=True)
    power = jnp.floor(jnp.log2(jnp.maximum(peak, 1e-30)) + 1.001)
    code = jnp.clip(jnp.round(value * jnp.exp2(15.0 - power)), -32767.0, 32767.0)
    code = code.astype(jnp.int32).astype(jnp.int16)
    power = jnp.broadcast_to(power, (EDGE, WIDTH)).astype(jnp.int32).astype(jnp.int16)
    for place in places:
        coded[place, 0:rows] = code
        coded[place, rows : rows + EDGE] = power


def decode(coded):
    rows = coded.shape[0] - EDGE
    power = coded[rows:].astype(jnp.int32).astype(jnp.float32)[0:1]
    return coded[:rows].astype(jnp.int32).astype(jnp.float32) * jnp.exp2(power - 15.0)


def encode_half_kernel(mine, theirs, coded):
    chunk = coded.shape[1] - EDGE
    for n in range(coded.shape[0]):
        encode(mine[n * chunk : n * chunk + chunk] + decode(theirs[n]), coded, (n,))


def sum_kernel(scale, coded, again):
    total = decode(coded[0])
    for n in range(1, coded.shape[0]):
        total = total + decode(coded[n])
    encode(total * scale, again, range(again.shape[0]))


def decode_kernel(flip, core, coded, *refs):
    out, part, done = refs[-3:]
    chunk = coded.shape[1] - EDGE
    here = core[0] + flip * (1 - 2 * core[0])
    copies = []
    for n in range(coded.shape[0]):
        rows = min(chunk, HALF - n * chunk)
        spot = pl.ds(n * chunk, rows)
        part[spot] = decode(coded[n])[0:rows]
        target = out.at[pl.ds(pl.multiple_of(here * HALF + n * chunk, EDGE), rows)]
        copies.append(pltpu.make_async_copy(part.at[spot], target, done.at[n]))
        copies[-1].start()
    for copy in copies:
        copy.wait()


SMEM = pl.BlockSpec(memory_space=pltpu.SMEM)
VMEM = pl.BlockSpec(memory_space=pltpu.VMEM)


def call(kernel, name, out_shape, scratch=(), scalars=0, flops=0, nbytes=4 << 20):
    def run(*args):
        return pl.pallas_call(
            kernel,
            out_shape=out_shape,
            in_specs=[SMEM] * scalars + [VMEM] * (len(args) - scalars),
            out_specs=jax.tree.map(lambda _: VMEM, out_shape),
            scratch_shapes=list(scratch),
            compiler_params=pltpu.CompilerParams(vmem_limit_bytes=20 << 20),
            cost_estimate=pl.CostEstimate(flops=flops, bytes_accessed=nbytes, transcendentals=0),
            name=name,
        )(*args)

    return run


def features_call(i, args, scratch, flops, before=None):
    grad = args[2]
    block = (EDGE,) + grad.shape[1:]
    specs = [SMEM, SMEM] + [VMEM] * (len(args) - 2)
    if before is not None:
        args = args + (before,)
        specs.append(pl.BlockSpec(memory_space=pl.ANY))
    return pl.pallas_call(
        lambda *refs: feature_kernel(i, *refs),
        grid=(1,),
        out_shape=jax.ShapeDtypeStruct(grad.shape, jnp.bfloat16),
        in_specs=specs,
        out_specs=pl.BlockSpec(block, lambda g: (i, 0, 0, 0, 0)),
        scratch_shapes=list(scratch),
        input_output_aliases={} if before is None else {len(args) - 1: 0},
        compiler_params=pltpu.CompilerParams(vmem_limit_bytes=20 << 20),
        cost_estimate=pl.CostEstimate(flops=flops, bytes_accessed=4 << 20, transcendentals=0),
        name="conv_features",
    )(*args)


def pack_edges(occ, grad):
    row = (1,) + grad.shape[1:]
    tile = (1,) + occ.shape[1:]
    ends = (0, grad.shape[0] - 1)
    tiles = [pl.BlockSpec(tile, lambda g, at=at: (at, 0, 0, 0)) for at in ends]
    rows = [pl.BlockSpec(row, lambda g, at=at: (at, 0, 0, 0, 0)) for at in ends]
    return pl.pallas_call(
        pack_kernel,
        grid=(1,),
        out_shape=[jax.ShapeDtypeStruct(row, jnp.bfloat16)] * 2,
        in_specs=tiles + rows,
        out_specs=[pl.BlockSpec(row, lambda g: (0, 0, 0, 0, 0))] * 2,
        cost_estimate=pl.CostEstimate(flops=0, bytes_accessed=1 << 18, transcendentals=0),
        name="pack_edges",
    )(occ, occ, grad, grad)


def decode_part(core, coded, *before):
    anywhere = pl.BlockSpec(memory_space=pl.ANY)
    flip = len(before)
    return pl.pallas_call(
        lambda *refs: decode_kernel(flip, *refs),
        in_specs=[SMEM, VMEM] + [anywhere] * flip,
        out_specs=anywhere,
        out_shape=jax.ShapeDtypeStruct((2 * HALF, WIDTH), jnp.float32),
        scratch_shapes=[pltpu.VMEM((HALF, WIDTH), jnp.float32), pltpu.SemaphoreType.DMA((coded.shape[0],))],
        input_output_aliases={2: 0} if before else {},
        compiler_params=pltpu.CompilerParams(vmem_limit_bytes=20 << 20),
        cost_estimate=pl.CostEstimate(flops=0, bytes_accessed=3 << 19, transcendentals=0),
        name="decode_half",
    )(core, coded, *before)


def exchange(blocks, axis):
    return lax.all_to_all(blocks, axis, 0, 0)


def local(features, grad_out, occupancy, leaf_z, neighbours, kernel):
    nx, ny = grad_out.shape[1], grad_out.shape[2]
    grad = grad_out[0]
    feat = features[0]
    occ = jnp.transpose(occupancy[0], (0, 2, 3, 1))
    gx, gy = lax.axis_size("gx"), lax.axis_size("gy")
    core = lax.axis_index("dcn").astype(jnp.int32).reshape(1)
    scale = 1.0 / math.sqrt(lax.axis_size("dcn") * gx * gy * nx * ny * 2 * EDGE)
    field = pltpu.VMEM((VIEW, ny + 2, 3, EDGE, WIDTH), jnp.float32)
    masks = pltpu.VMEM((VIEW, ny, 2, EDGE, WIDTH), jnp.float32)
    view = pltpu.VMEM((3, VIEW, VIEW, ROWS, WIDTH), jnp.bfloat16)
    own = pltpu.VMEM((EDGE, EDGE * ROWS, WIDTH), jnp.bfloat16)
    acc = pltpu.VMEM((UNIT, WIDTH), jnp.float32)
    strip = pltpu.VMEM((2, ny + 2, 3, EDGE, WIDTH), jnp.float32)
    row_view = pltpu.VMEM((3, VIEW, ROWS, WIDTH), jnp.bfloat16)
    product = 2 * 2 * 512 * 27 * WIDTH * WIDTH

    def shift(block, axis, step):
        count = lax.axis_size(axis)
        pairs = [(i, i + step) for i in range(count) if 0 <= i + step < count]
        return lax.ppermute(block, axis, pairs)

    def coded(count):
        return jax.ShapeDtypeStruct((count, PADDED // gy + EDGE, WIDTH), jnp.int16)

    def terms_of(i, *before):
        return call(
            lambda *refs: terms_kernel(i, *refs),
            "conv_terms",
            jax.ShapeDtypeStruct((2, PADDED, WIDTH), jnp.float32),
            (field, masks, view, own, strip, row_view),
            scalars=2,
            flops=product,
        )(neighbours, leaf_z, grad, feat, occ, *before)

    core, packed = lax.optimization_barrier((core, pack_edges(occ, grad)))
    last, first = packed
    top = shift(last, "gx", 1)
    bottom = shift(first, "gx", -1)
    own_side = jax.ShapeDtypeStruct((nx, 1, 2, EDGE, WIDTH), jnp.bfloat16)
    end, start = call(own_sides_kernel, "own_sides", (own_side, own_side), nbytes=1 << 19)(occ, grad)
    terms = terms_of(0)
    top, bottom, terms = lax.optimization_barrier((top, bottom, terms))
    side = jax.ShapeDtypeStruct((nx + 2, 1, 2, EDGE, WIDTH), jnp.bfloat16)
    end, start = call(sides_kernel, "pack_sides", (side, side), nbytes=1 << 17)(top, bottom, end, start)
    left = shift(end, "gy", 1)
    right = shift(start, "gy", -1)
    terms = terms_of(1, top, bottom, terms)
    edges = (top, bottom, left, right)
    mine, theirs, halo = call(
        edge_kernel,
        "edge_terms",
        (
            jax.ShapeDtypeStruct((PADDED, WIDTH), jnp.float32),
            coded(gy),
            jax.ShapeDtypeStruct((2 * (nx + ny + 2), 2, EDGE, WIDTH), jnp.bfloat16),
        ),
        (
            pltpu.VMEM((2, PADDED, WIDTH), jnp.float32),
            pltpu.VMEM((2, nx + 2, 3, EDGE, WIDTH), jnp.float32),
            pltpu.VMEM((3, VIEW, EDGE, WIDTH), jnp.float32),
        ),
        scalars=3,
        flops=product // 4,
    )(neighbours, leaf_z, core, feat, occ, *edges, terms)
    theirs = lax.ppermute(theirs, "dcn", [(0, 1), (1, 0)])
    half = call(encode_half_kernel, "encode_half", coded(gy), nbytes=2 << 20)(mine, theirs)

    def features_part(i, value, *before):
        late, value = lax.optimization_barrier((grad, value))
        args = (neighbours, leaf_z, late, occ, halo, kernel)
        return features_call(i, args, (field, masks, view, acc), product, *before), value

    half = exchange(half, "gy")
    piece = call(lambda c, o: sum_kernel(1.0, c, o), "sum_piece", coded(gx), nbytes=1 << 20)(half)
    out, piece = features_part(0, piece)
    piece, out = lax.optimization_barrier((exchange(piece, "gx"), out))
    total = call(lambda c, o: sum_kernel(scale, c, o), "sum_total", coded(gy), nbytes=1 << 20)(piece)
    out, total = features_part(1, total, out)
    total, out = lax.optimization_barrier((exchange(total, "gy"), out))
    other = lax.ppermute(total, "dcn", [(0, 1), (1, 0)])
    kernel_grad = decode_part(core, other, decode_part(core, total))
    return out[None], kernel_grad.reshape(27, WIDTH, WIDTH)


def solution(mesh):
    return jax.shard_map(
        local,
        mesh=mesh,
        in_specs=(
            P("dcn", "gx", "gy", None, None, None),
            P("dcn", "gx", "gy", None, None, None),
            P("dcn", "gx", "gy", None, None),
            P("dcn", "gx", "gy", None),
            P("dcn", "gx", "gy", None, None),
            P(),
        ),
        out_specs=(P("dcn", "gx", "gy", None, None, None), P()),
        check_vma=False,
    )
```
